256 devices in a mesh: inst: 8 (over x, core), lab: 32 (over z, y).
Axes of the slice: x: 4, y: 4, z: 8, core: 2. Of those that a mesh axis runs over, the one named last changes fastest.
Arguments:
- features: bfloat16 [4096, 768], P('inst'), may hold values from -6 to 6
- tile_rows: int32 [2048], P(('inst', 'lab')), may hold values from 0 to 1, as said below
- tile_labels: int32 [2048], P(('inst', 'lab')), may hold values from 0 to 7
- tile_values: bfloat16 [2048, 256, 256], P(('inst', 'lab')), may hold values from 0 to 1
- cluster_ids: int32 [65536], P(('lab', 'inst')), may hold values from 0 to 8191, as said below
Outputs:
- label_embed: float32 [65536, 768], P(('lab', 'inst'))
- centroids: float32 [8192, 768], P(('inst', 'lab'))
The draws below stay inside these ranges and needn't reach their ends.
Inputs may be any that keep to these rules, and one draw needn't show every extreme that they name: Within each block of 8 entries the pairs (tile_rows, tile_labels) are distinct. Within each aligned block of 256 labels, at most 2 labels have clusters with the same value of cluster_ids // 32, and that many is reached in every block.
All inputs are finite; a program needn't handle non-finite values.
Results may differ from the reference program's by a relative error of at most 0.01.
Values may be sent and summed in bfloat16 or wider, within the bound.
No kernel may reach another device: no remote copies, remote signals or barrier semaphores. Data moves between devices by JAX's collectives and lax.ppermute only.
A program may use at most 128 MiB of HBM per device.

```python
import jax
import jax.numpy as jnp
from jax import lax

D = 768
TILE = 256
INST_DEV = 512
LAB_DEV = 256
CL_OWN = 32
OWNERS = 256
RT = 2
LT = 8
NT_DEV = 8
TILES = 2048
INSTANCES = 4096
CLUST = 8192
N_INST = 8
N_LAB = 32


def tile_pairs(key):
    keys = jax.random.split(jax.random.fold_in(key, 17), OWNERS)

    def pick(single):
        return jax.random.permutation(single, RT * LT)[:NT_DEV]
    picks = jax.vmap(pick)(keys).reshape(-1).astype(jnp.int32)
    return (picks // LT, picks % LT)


def draw_tile_rows(key, part):
    return tile_pairs(key)[0]


def draw_tile_labels(key, part):
    return tile_pairs(key)[1]


def draw_cluster_ids(key, part):
    keys = jax.random.split(jax.random.fold_in(key, 5), OWNERS)
    lowest = max(1, OWNERS // 16)

    def block(single):
        first, second, third, fourth = jax.random.split(single, 4)
        order = jax.random.permutation(first, OWNERS).astype(jnp.int32)
        doubled = jax.random.randint(second, (), lowest, OWNERS // 2 + 1)
        ranks = jnp.arange(LAB_DEV, dtype=jnp.int32) % OWNERS
        ranks = jnp.where(ranks >= OWNERS - doubled, ranks - (OWNERS - doubled), ranks)
        owner = order[ranks]
        inside = jax.random.randint(third, (LAB_DEV,), 0, CL_OWN)
        return jax.random.permutation(fourth, owner * CL_OWN + inside)
    return jax.vmap(block)(keys).reshape(-1).astype(jnp.int32)


def block_scale(own_key, dims, cuts, least, largest):
    def one(axis_at, blocks):
        steps = jax.random.uniform(jax.random.fold_in(jax.random.fold_in(own_key, 6), axis_at), (blocks,), jnp.float32, least / len(cuts), largest / len(cuts))
        return jnp.repeat(jnp.exp(steps), dims[axis_at] // blocks).reshape((-1,) + (1,) * (len(dims) - axis_at - 1))

    level = one(*cuts[0])
    for cut in cuts[1:]:
        level = level * one(*cut)
    return level


def normal_values(own_key, extent, width, reach, cuts=(), kind=jnp.bfloat16):
    level = block_scale(own_key, extent, cuts, -0.22, 0.18) if cuts else 1.0
    values = jax.random.normal(own_key, extent, jnp.float32) * width * level
    return jnp.minimum(jnp.maximum(values, -reach), reach).astype(kind)


def setup_inputs(seed: int = 0) -> dict:
    seeds = jax.random.split(jax.random.key(seed), 6)
    features = normal_values(seeds[0], (INSTANCES, D), 1.0, 6.0, ((0, 8),))
    tile_rows = draw_tile_rows(jax.random.fold_in(seeds[5], 71), 0)
    tile_labels = draw_tile_labels(jax.random.fold_in(seeds[5], 71), 0)
    tile_values = jnp.clip(1.0 * jax.random.uniform(seeds[3], (TILES, TILE, TILE), jnp.float32) ** block_scale(seeds[3], (TILES, TILE, TILE), ((0, 256),), -0.2, 0.2), 0.0, 1.0).astype(jnp.bfloat16)
    cluster_ids = draw_cluster_ids(jax.random.fold_in(seeds[5], 71), 0)
    return {"features": features, "tile_rows": tile_rows, "tile_labels": tile_labels, "tile_values": tile_values, "cluster_ids": cluster_ids}


def unit_rows(matrix):
    return matrix * lax.rsqrt(lax.optimization_barrier(jnp.sum(matrix * matrix, axis=-1, keepdims=True)) + 1e-06)

def reference(features, tile_rows, tile_labels, tile_values, cluster_ids):
    normed = unit_rows(features.astype(jnp.float32)).astype(jnp.bfloat16)
    row_tiles = INST_DEV // TILE
    lab_tiles = LAB_DEV * N_INST // TILE
    block_rows = LAB_DEV * N_INST
    shard_x = normed.reshape(N_INST, row_tiles, TILE, D)
    rows_all = tile_rows.reshape(N_INST, N_LAB, NT_DEV)
    labs_all = tile_labels.reshape(N_INST, N_LAB, NT_DEV)
    vals_all = tile_values.reshape(N_INST, N_LAB, NT_DEV, TILE, TILE)

    def shard_step(carry, pieces):
        xs, rr, cc, vv = pieces

        def one_block(parts):
            row_ids, lab_ids, values = parts
            picked = xs[row_ids].astype(jnp.float32)
            prod = jnp.einsum('nrl,nrd->nld', values.astype(jnp.float32), picked)
            seg = jax.ops.segment_sum(prod, lab_ids, num_segments=lab_tiles)
            return seg.reshape(block_rows, D).astype(jnp.bfloat16)
        partial_value = lax.map(one_block, (rr, cc, vv))
        return (carry + partial_value.astype(jnp.float32), None)
    start = jnp.zeros((N_LAB, block_rows, D), jnp.float32)
    summed, _ = lax.scan(shard_step, start, (shard_x, rows_all, labs_all, vals_all))
    label_embed = unit_rows(summed.reshape(N_LAB * block_rows, D))
    cluster_sums = jax.ops.segment_sum(label_embed, cluster_ids, num_segments=CLUST)
    return (label_embed, unit_rows(cluster_sums))
```

```python
import functools

import jax
import jax.numpy as jnp
from jax import lax
from jax.experimental import pallas as pl
from jax.experimental.pallas import tpu as pltpu
from jax.sharding import PartitionSpec as P

CL_OWN = 32
TILE = 256
SLOTS = 2
LANES = 128
BF = jnp.bfloat16
F32 = jnp.float32


def full(shape):
    return pl.BlockSpec(shape, lambda *_: (0,) * len(shape))


def tiles_in(rows_hbm, labs_hbm, vals_hbm, rows_ref, labs_ref, vals_ref, sems):
    pairs = ((rows_hbm, rows_ref), (labs_hbm, labs_ref), (vals_hbm, vals_ref))
    return [pltpu.make_async_copy(src, dst, sems.at[k]) for k, (src, dst) in enumerate(pairs)]


def half_product(other, chips, rows_ref, labs_ref, vals_ref, x_ref, out_ref, acc_ref):
    tiles, tile = vals_ref.shape[0], vals_ref.shape[1]
    me = lax.axis_index("inst")
    core = lax.rem(me, 2)
    chip = lax.div(me, 2)
    if other:
        core = 1 - core
    for d in range(chips):
        lab = lax.rem(chip + d, chips) * 2 + core
        acc_ref[...] = jnp.zeros_like(acc_ref)
        for r in range(x_ref.shape[0] // tile):
            n = jnp.int32(-1)
            for t in range(tiles):
                n = jnp.where((rows_ref[t] == r) & (labs_ref[t] == lab), t, n)

            @pl.when(n >= 0)
            def _(n=n, r=r):
                acc_ref[...] += lax.dot_general(
                    vals_ref[n],
                    x_ref[r * tile : (r + 1) * tile, :],
                    (((0,), (0,)), ((), ())),
                    preferred_element_type=F32,
                )

        out_ref[d * tile : (d + 1) * tile, :] = acc_ref[...].astype(BF)


def first_kernel(
    chips, rows_hbm, labs_hbm, vals_hbm, feat_hbm, out_ref, x_ref, rows_ref, labs_ref, vals_ref, feat_ref, acc_ref, sems
):
    feat_in = pltpu.make_async_copy(feat_hbm, feat_ref, sems.at[3])
    copies = tiles_in(rows_hbm, labs_hbm, vals_hbm, rows_ref, labs_ref, vals_ref, sems)
    feat_in.start()
    for copy in copies:
        copy.start()
    feat_in.wait()
    f = feat_ref[...].astype(F32)
    x_ref[...] = (f * lax.rsqrt(jnp.sum(f * f, axis=-1, keepdims=True) + 1e-06)).astype(BF)
    for copy in copies:
        copy.wait()
    half_product(True, chips, rows_ref, labs_ref, vals_ref, x_ref, out_ref, acc_ref)


def second_kernel(chips, rows_hbm, labs_hbm, vals_hbm, x_ref, out_ref, rows_ref, labs_ref, vals_ref, acc_ref, sems):
    copies = tiles_in(rows_hbm, labs_hbm, vals_hbm, rows_ref, labs_ref, vals_ref, sems)
    for copy in copies:
        copy.start()
    for copy in copies:
        copy.wait()
    half_product(False, chips, rows_ref, labs_ref, vals_ref, x_ref, out_ref, acc_ref)


def pack_kernel(own_ref, mate_ref, a_ref, b_ref, c_ref, ids_ref, emb_ref, out_ref, stage_ref):
    labs, width = emb_ref.shape
    cols = width // LANES
    step = (cols + 1) * SLOTS
    summed = own_ref[...].astype(F32) + mate_ref[...].astype(F32)
    summed = summed + a_ref[...].astype(F32) + b_ref[...].astype(F32) + c_ref[...].astype(F32)
    unit = summed * lax.rsqrt(jnp.sum(summed * summed, axis=-1, keepdims=True) + 1e-06)
    emb_ref[...] = unit
    unit = unit.astype(BF)
    ids = ids_ref[...]
    down = lax.broadcasted_iota(jnp.int32, (labs, labs), 0)
    across = lax.broadcasted_iota(jnp.int32, (labs, labs), 1)
    ids_down = jnp.sum(jnp.where(down == across, ids, 0), axis=1, keepdims=True)
    owner = ids // CL_OWN
    earlier = (ids_down // CL_OWN == owner) & (down < across)
    rank = jnp.sum(earlier.astype(jnp.int32), axis=0, keepdims=True)
    inside = jnp.broadcast_to((ids_down % CL_OWN).astype(F32), (labs, LANES)).astype(BF)
    for slot in range(SLOTS):
        pick = jnp.where((down == owner) & (rank == slot), 1.0, 0.0).astype(BF)
        moved = jnp.dot(pick, unit, preferred_element_type=F32)
        for col in range(cols):
            stage_ref[pl.ds(col * SLOTS + slot, labs, stride=step), :] = moved[:, col * LANES : (col + 1) * LANES]
        stage_ref[pl.ds(cols * SLOTS + slot, labs, stride=step), :] = jnp.dot(
            pick, inside, preferred_element_type=F32
        )
    out_ref.reshape(labs * step, LANES)[...] = stage_ref[...].astype(BF)


def combine_kernel(got_ref, out_ref, stage_ref):
    owners, cols = got_ref.shape[0], got_ref.shape[1] - 1
    step = (cols + 1) * SLOTS
    stage_ref[...] = got_ref.reshape(owners * step, LANES)[...].astype(F32)
    lane = lax.broadcasted_iota(jnp.int32, (owners, LANES), 1).astype(F32)
    total = jnp.zeros((LANES, cols * LANES), F32)
    for slot in range(SLOTS):
        inside = stage_ref[pl.ds(cols * SLOTS + slot, owners, stride=step), :]
        member = jnp.where(inside == lane, 1.0, 0.0).astype(BF)
        rows = jnp.concatenate(
            [stage_ref[pl.ds(col * SLOTS + slot, owners, stride=step), :].astype(BF) for col in range(cols)], axis=1
        )
        total = total + lax.dot_general(member, rows, (((0,), (0,)), ((), ())), preferred_element_type=F32)
    sums = total[:CL_OWN]
    out_ref[...] = sums * lax.rsqrt(jnp.sum(sums * sums, axis=-1, keepdims=True) + 1e-06)


def shards(features, tile_rows, tile_labels, tile_values, cluster_ids):
    tiles, tile = tile_values.shape[:2]
    insts, width = features.shape
    labs = cluster_ids.shape[0]
    n_inst = lax.axis_size("inst")
    owners = lax.axis_size(("inst", "lab"))
    chips = n_inst // 2
    cols = width // LANES
    hbm = pl.BlockSpec(memory_space=pltpu.MemorySpace.HBM)
    features, tile_rows, tile_labels, tile_values = (
        pltpu.with_memory_space_constraint(a, pltpu.MemorySpace.HBM)
        for a in (features, tile_rows, tile_labels, tile_values)
    )
    half = jax.ShapeDtypeStruct((chips * tile, width), BF)
    cost = pl.CostEstimate(
        flops=tiles * tile * tile * width, bytes_accessed=2 * (chips + 2) * tile * width, transcendentals=0
    )
    tile_scratch = [pltpu.SMEM((tiles,), jnp.int32)] * 2 + [pltpu.VMEM(tile_values.shape, BF)]
    away, normed = pl.pallas_call(
        functools.partial(first_kernel, chips),
        grid=(1,),
        out_shape=(half, jax.ShapeDtypeStruct((insts, width), BF)),
        in_specs=[hbm] * 4,
        out_specs=(full(half.shape), full((insts, width))),
        scratch_shapes=tile_scratch
        + [pltpu.VMEM((insts, width), BF), pltpu.VMEM((tile, width), F32), pltpu.SemaphoreType.DMA((4,))],
        compiler_params=pltpu.CompilerParams(vmem_limit_bytes=24 << 20),
        cost_estimate=cost,
        name="away_half",
    )(tile_rows, tile_labels, tile_values, features)
    mate = lax.ppermute(away, "inst", [(i, i ^ 1) for i in range(n_inst)])
    own = pl.pallas_call(
        functools.partial(second_kernel, chips),
        grid=(1,),
        out_shape=half,
        in_specs=[hbm] * 3 + [full((insts, width))],
        out_specs=full(half.shape),
        scratch_shapes=tile_scratch + [pltpu.VMEM((tile, width), F32), pltpu.SemaphoreType.DMA((3,))],
        compiler_params=pltpu.CompilerParams(vmem_limit_bytes=24 << 20),
        cost_estimate=cost,
        name="own_half",
    )(tile_rows, tile_labels, tile_values, normed)
    arrived = []
    for d in (1, 3, 2):
        part = slice(d * tile, (d + 1) * tile)
        block = (own[part].astype(F32) + mate[part].astype(F32)).astype(BF)
        arrived.append(lax.ppermute(block, "inst", [(i, (i + 2 * d) % n_inst) for i in range(n_inst)]))
    block = full((tile, width))
    message = (owners, cols + 1, SLOTS, LANES)
    label_embed, packed = pl.pallas_call(
        pack_kernel,
        grid=(1,),
        out_shape=(jax.ShapeDtypeStruct((labs, width), F32), jax.ShapeDtypeStruct(message, BF)),
        in_specs=[block] * 5 + [full((1, labs))],
        out_specs=(full((labs, width)), full(message)),
        scratch_shapes=[pltpu.VMEM((owners * (cols + 1) * SLOTS, LANES), F32)],
        compiler_params=pltpu.CompilerParams(vmem_limit_bytes=24 << 20),
        name="pack",
    )(own, mate, *arrived, cluster_ids.reshape(1, labs))
    got = lax.all_to_all(packed, ("inst", "lab"), 0, 0, tiled=True)
    centroids = pl.pallas_call(
        combine_kernel,
        grid=(1,),
        out_shape=jax.ShapeDtypeStruct((CL_OWN, width), F32),
        in_specs=[full(message)],
        out_specs=full((CL_OWN, width)),
        scratch_shapes=[pltpu.VMEM((owners * (cols + 1) * SLOTS, LANES), F32)],
        compiler_params=pltpu.CompilerParams(vmem_limit_bytes=24 << 20),
        name="combine",
    )(got)
    return label_embed, centroids


def solution(mesh):
    return jax.shard_map(
        shards,
        mesh=mesh,
        in_specs=(
            P("inst", None),
            P(("inst", "lab")),
            P(("inst", "lab")),
            P(("inst", "lab"), None, None),
            P(("lab", "inst")),
        ),
        out_specs=(P(("lab", "inst"), None), P(("inst", "lab"), None)),
        check_vma=False,
    )
```

```python
import functools

import jax
import jax.numpy as jnp
from jax import lax
from jax.experimental import pallas as pl
from jax.experimental.pallas import tpu as pltpu
from jax.sharding import Mesh
from jax.sharding import PartitionSpec as P

CL_OWN = 32
SLOTS = 2
LANES = 128
CORES = 2
Y_CHIPS = 4
INST = ("x", "c")
LAB = ("z", "y")
BF = jnp.bfloat16
F32 = jnp.float32


def full(shape):
    return pl.BlockSpec(shape, lambda *_: (0,) * len(shape))


def params(**kwargs):
    return pltpu.CompilerParams(vmem_limit_bytes=24 << 20, **kwargs)


def in_hbm(array):
    return pltpu.with_memory_space_constraint(array, pltpu.MemorySpace.HBM)


def tiles_in(rows_hbm, labs_hbm, vals_hbm, rows_ref, labs_ref, vals_ref, sems):
    pairs = ((rows_hbm, rows_ref), (labs_hbm, labs_ref), (vals_hbm, vals_ref))
    return [pltpu.make_async_copy(src, dst, sems.at[k]) for k, (src, dst) in enumerate(pairs)]


def product(other, steps, rows_ref, labs_ref, vals_ref, x_ref, out_ref, acc_ref):
    tiles, tile = vals_ref.shape[0], vals_ref.shape[1]
    core = lax.axis_index("c")
    if other:
        core = 1 - core
    for k, step in enumerate(steps):
        lab = lax.rem(lax.axis_index("x") + step, lax.axis_size("x")) * CORES + core
        acc_ref[...] = jnp.zeros_like(acc_ref)
        for r in range(x_ref.shape[0] // tile):
            n = jnp.int32(-1)
            for t in range(tiles):
                n = jnp.where((rows_ref[t] == r) & (labs_ref[t] == lab), t, n)

            @pl.when(n >= 0)
            def _(n=n, r=r):
                acc_ref[...] += lax.dot_general(
                    vals_ref[n],
                    x_ref[r * tile : (r + 1) * tile, :],
                    (((0,), (0,)), ((), ())),
                    preferred_element_type=F32,
                )

        out_ref[k * tile : (k + 1) * tile, :] = acc_ref[...].astype(BF)


def first_kernel(
    steps, rows_hbm, labs_hbm, vals_hbm, feat_hbm, out_ref, x_ref, rows_ref, labs_ref, vals_ref, feat_ref, acc_ref, sems
):
    feat_in = pltpu.make_async_copy(feat_hbm, feat_ref, sems.at[3])
    copies = tiles_in(rows_hbm, labs_hbm, vals_hbm, rows_ref, labs_ref, vals_ref, sems)
    feat_in.start()
    for copy in copies:
        copy.start()
    feat_in.wait()
    f = feat_ref[...].astype(F32)
    x_ref[...] = (f * lax.rsqrt(jnp.sum(f * f, axis=-1, keepdims=True) + 1e-06)).astype(BF)
    for copy in copies:
        copy.wait()
    product(True, steps, rows_ref, labs_ref, vals_ref, x_ref, out_ref, acc_ref)


def later_kernel(jobs, rows_hbm, labs_hbm, vals_hbm, x_ref, *refs):
    out_refs, (rows_ref, labs_ref, vals_ref, acc_ref, sems) = refs[: len(jobs)], refs[len(jobs) :]
    copies = tiles_in(rows_hbm, labs_hbm, vals_hbm, rows_ref, labs_ref, vals_ref, sems)
    for copy in copies:
        copy.start()
    for copy in copies:
        copy.wait()
    for (other, steps), out_ref in zip(jobs, out_refs):
        product(other, steps, rows_ref, labs_ref, vals_ref, x_ref, out_ref, acc_ref)


def route_kernel(ids_ref, place_ref, inside_ref):
    slots, owners, labs = place_ref.shape
    ids = ids_ref[...]
    down = lax.broadcasted_iota(jnp.int32, (labs, labs), 0)
    across = lax.broadcasted_iota(jnp.int32, (labs, labs), 1)
    ids_down = jnp.sum(jnp.where(down == across, ids, 0), axis=1, keepdims=True)
    owner = ids // CL_OWN
    earlier = (ids_down // CL_OWN == owner) & (down < across)
    rank = jnp.sum(earlier.astype(jnp.int32), axis=0, keepdims=True)
    here = lax.broadcasted_iota(jnp.int32, (owners, labs), 0) == owner
    for slot in range(slots):
        place_ref[slot] = jnp.where(here & (rank == slot), 1.0, 0.0).astype(BF)
    inside_ref[...] = jnp.broadcast_to((ids_down % CL_OWN).astype(F32), inside_ref.shape).astype(BF)


def ring_kernel(own_ref, mate_ref, up_ref, down_ref, plus_ref, minus_ref):
    tile = plus_ref.shape[0]
    half = tile // 2

    def pair(start):
        return own_ref[start : start + half].astype(F32) + mate_ref[start : start + half].astype(F32)

    plus_ref[:half] = (pair(tile) + up_ref[...].astype(F32)).astype(BF)
    plus_ref[half:] = pair(tile + half).astype(BF)
    minus_ref[:half] = pair(2 * tile).astype(BF)
    minus_ref[half:] = (pair(2 * tile + half) + down_ref[...].astype(F32)).astype(BF)


def pack_kernel(own_ref, mate_ref, a_ref, b_ref, place_ref, inside_ref, emb_ref, out_ref, stage_ref):
    width = emb_ref.shape[1]
    slots, owners = place_ref.shape[:2]
    cols = width // LANES
    step = (cols + 1) * slots
    summed = own_ref[...].astype(F32) + mate_ref[...].astype(F32)
    summed = summed + a_ref[...].astype(F32) + b_ref[...].astype(F32)
    unit = summed * lax.rsqrt(jnp.sum(summed * summed, axis=-1, keepdims=True) + 1e-06)
    emb_ref[...] = unit
    unit = unit.astype(BF)
    for slot in range(slots):
        moved = jnp.dot(place_ref[slot], unit, preferred_element_type=F32)
        for col in range(cols):
            stage_ref[pl.ds(col * slots + slot, owners, stride=step), :] = moved[:, col * LANES : (col + 1) * LANES]
        stage_ref[pl.ds(cols * slots + slot, owners, stride=step), :] = jnp.dot(
            place_ref[slot], inside_ref[...], preferred_element_type=F32
        )
    out_ref.reshape(owners * step, LANES)[...] = stage_ref[...].astype(BF)


def combine_kernel(got_ref, out_ref, stage_ref):
    owners, cols = got_ref.shape[0], got_ref.shape[1] - 1
    step = (cols + 1) * SLOTS
    stage_ref[...] = got_ref.reshape(owners * step, LANES)[...].astype(F32)
    lane = lax.broadcasted_iota(jnp.int32, (owners, LANES), 1).astype(F32)
    total = jnp.zeros((LANES, cols * LANES), F32)
    for slot in range(SLOTS):
        inside = stage_ref[pl.ds(cols * SLOTS + slot, owners, stride=step), :]
        member = jnp.where(inside == lane, 1.0, 0.0).astype(BF)
        rows = jnp.concatenate(
            [stage_ref[pl.ds(col * SLOTS + slot, owners, stride=step), :].astype(BF) for col in range(cols)], axis=1
        )
        total = total + lax.dot_general(member, rows, (((0,), (0,)), ((), ())), preferred_element_type=F32)
    sums = total[:CL_OWN]
    out_ref[...] = sums * lax.rsqrt(jnp.sum(sums * sums, axis=-1, keepdims=True) + 1e-06)


def shards(features, tile_rows, tile_labels, tile_values, cluster_ids):
    features, tile_rows, tile_labels, tile_values = (
        in_hbm(a) for a in (features, tile_rows, tile_labels, tile_values)
    )
    tiles, tile = tile_values.shape[:2]
    insts, width = features.shape
    labs = cluster_ids.shape[0]
    chips = lax.axis_size("x")
    owners = lax.axis_size(INST + LAB)
    cols = width // LANES
    hbm = pl.BlockSpec(memory_space=pltpu.MemorySpace.HBM)
    tile_scratch = [pltpu.SMEM((tiles,), jnp.int32)] * 2 + [pltpu.VMEM(tile_values.shape, BF)]
    far_steps, near_steps = (2,), (0, 1, 3)

    def product_cost(steps):
        return pl.CostEstimate(
            flops=len(steps) * tile * tile * width * 2,
            bytes_accessed=2 * (tiles * tile * tile + insts * width + len(steps) * tile * width),
            transcendentals=0,
        )

    far_away, normed = pl.pallas_call(
        functools.partial(first_kernel, far_steps),
        grid=(1,),
        out_shape=(jax.ShapeDtypeStruct((tile, width), BF), jax.ShapeDtypeStruct((insts, width), BF)),
        in_specs=[hbm] * 4,
        out_specs=(full((tile, width)), full((insts, width))),
        scratch_shapes=tile_scratch
        + [pltpu.VMEM((insts, width), BF), pltpu.VMEM((tile, width), F32), pltpu.SemaphoreType.DMA((4,))],
        compiler_params=params(),
        cost_estimate=product_cost(far_steps),
        name="far_away",
    )(tile_rows, tile_labels, tile_values, features)

    def later(name, x, *jobs):
        shapes = [(len(steps) * tile, width) for _, steps in jobs]
        return pl.pallas_call(
            functools.partial(later_kernel, jobs),
            grid=(1,),
            out_shape=[jax.ShapeDtypeStruct(shape, BF) for shape in shapes],
            in_specs=[hbm] * 3 + [full((insts, width))],
            out_specs=[full(shape) for shape in shapes],
            scratch_shapes=tile_scratch + [pltpu.VMEM((tile, width), F32), pltpu.SemaphoreType.DMA((3,))],
            compiler_params=params(),
            cost_estimate=product_cost(sum((steps for _, steps in jobs), ())),
            name=name,
        )(tile_rows, tile_labels, tile_values, x)

    def across(block):
        return lax.ppermute(block, "c", [(0, 1), (1, 0)])

    def along(block, step):
        return lax.ppermute(block, "x", [(i, (i + step) % chips) for i in range(chips)])

    far_mate = across(far_away)
    far_own, near_away = later("far_own", normed, (False, far_steps), (True, near_steps))
    cut = tile // 2
    far = [(far_own[h].astype(F32) + far_mate[h].astype(F32)).astype(BF) for h in (slice(0, cut), slice(cut, tile))]
    ids, normed, near_away, far = lax.optimization_barrier((cluster_ids, normed, near_away, far))
    up = along(far[0], 1)
    down = along(far[1], -1)
    mate = across(near_away)
    (own,) = later("near_own", normed, (False, near_steps))
    place, inside = pl.pallas_call(
        route_kernel,
        grid=(1,),
        out_shape=(jax.ShapeDtypeStruct((SLOTS, owners, labs), BF), jax.ShapeDtypeStruct((labs, LANES), BF)),
        in_specs=[full((1, labs))],
        out_specs=(full((SLOTS, owners, labs)), full((labs, LANES))),
        compiler_params=params(),
        name="route",
    )(ids.reshape(1, labs))
    block = full((tile, width))
    plus, minus = pl.pallas_call(
        ring_kernel,
        grid=(1,),
        out_shape=[jax.ShapeDtypeStruct((tile, width), BF)] * 2,
        in_specs=[full(own.shape)] * 2 + [full((tile // 2, width))] * 2,
        out_specs=[block] * 2,
        compiler_params=params(),
        name="ring",
    )(own, mate, up, down)
    message = (owners, cols + 1, SLOTS, LANES)
    stage = pltpu.VMEM((owners * (cols + 1) * SLOTS, LANES), F32)
    label_embed, rows = pl.pallas_call(
        pack_kernel,
        grid=(1,),
        out_shape=(jax.ShapeDtypeStruct((labs, width), F32), jax.ShapeDtypeStruct(message, BF)),
        in_specs=[block] * 4 + [full((SLOTS, owners, labs)), full((labs, LANES))],
        out_specs=(full((labs, width)), full(message)),
        scratch_shapes=[stage],
        compiler_params=params(),
        name="pack",
    )(own, mate, along(plus, 1), along(minus, -1), place, inside)
    got = lax.all_to_all(rows, INST + LAB, 0, 0, tiled=True)
    centroids = pl.pallas_call(
        combine_kernel,
        grid=(1,),
        out_shape=jax.ShapeDtypeStruct((CL_OWN, width), F32),
        in_specs=[full(message)],
        out_specs=full((CL_OWN, width)),
        scratch_shapes=[stage],
        compiler_params=params(),
        name="combine",
    )(got)
    return label_embed, centroids


def solution(mesh):
    insts, labs = mesh.devices.shape
    cut = (insts // CORES, CORES, labs // Y_CHIPS, Y_CHIPS)
    return jax.shard_map(
        shards,
        mesh=Mesh(mesh.devices.reshape(cut), INST + LAB),
        in_specs=(P(INST, None), P(INST + LAB), P(INST + LAB), P(INST + LAB, None, None), P(LAB + INST)),
        out_specs=(P(LAB + INST, None), P(INST + LAB, None)),
        check_vma=False,
    )
```

```python
import functools

import jax
import jax.numpy as jnp
from jax import lax
from jax.experimental import pallas as pl
from jax.experimental.pallas import tpu as pltpu
from jax.sharding import Mesh
from jax.sharding import PartitionSpec as P

CL_OWN = 32
SLOTS = 2
LANES = 128
CORES = 2
Y_CHIPS = 4
INST = ("x", "c")
LAB = ("z", "y")
BF = jnp.bfloat16
F32 = jnp.float32


def full(shape):
    return pl.BlockSpec(shape, lambda *_: (0,) * len(shape))


def params(**kwargs):
    return pltpu.CompilerParams(vmem_limit_bytes=24 << 20, **kwargs)


def in_hbm(array):
    return pltpu.with_memory_space_constraint(array, pltpu.MemorySpace.HBM)


def tiles_in(rows_hbm, labs_hbm, vals_hbm, rows_ref, labs_ref, vals_ref, sems):
    pairs = ((rows_hbm, rows_ref), (labs_hbm, labs_ref), (vals_hbm, vals_ref))
    return [pltpu.make_async_copy(src, dst, sems.at[k]) for k, (src, dst) in enumerate(pairs)]


def product(other, steps, rows_ref, labs_ref, vals_ref, x_ref, out_ref, acc_ref):
    tiles, tile = vals_ref.shape[0], vals_ref.shape[1]
    chips = lax.axis_size("x")
    core = lax.axis_index("c")
    if other:
        core = 1 - core
    for k, step in enumerate(steps):
        lab = lax.rem(lax.axis_index("x") + step * (1 - 2 * core) + chips, chips) * CORES + core
        acc_ref[...] = jnp.zeros_like(acc_ref)
        for r in range(x_ref.shape[0] // tile):
            n = jnp.int32(-1)
            for t in range(tiles):
                n = jnp.where((rows_ref[t] == r) & (labs_ref[t] == lab), t, n)

            @pl.when(n >= 0)
            def _(n=n, r=r):
                acc_ref[...] += lax.dot_general(
                    vals_ref[n],
                    x_ref[r * tile : (r + 1) * tile, :],
                    (((0,), (0,)), ((), ())),
                    preferred_element_type=F32,
                )

        out_ref[k * tile : (k + 1) * tile, :] = acc_ref[...].astype(BF)


def first_kernel(
    steps, rows_hbm, labs_hbm, vals_hbm, feat_hbm, out_ref, x_ref, rows_ref, labs_ref, vals_ref, feat_ref, acc_ref, sems
):
    feat_in = pltpu.make_async_copy(feat_hbm, feat_ref, sems.at[3])
    copies = tiles_in(rows_hbm, labs_hbm, vals_hbm, rows_ref, labs_ref, vals_ref, sems)
    feat_in.start()
    for copy in copies:
        copy.start()
    feat_in.wait()
    f = feat_ref[...].astype(F32)
    x_ref[...] = (f * lax.rsqrt(jnp.sum(f * f, axis=-1, keepdims=True) + 1e-06)).astype(BF)
    for copy in copies:
        copy.wait()
    product(True, steps, rows_ref, labs_ref, vals_ref, x_ref, out_ref, acc_ref)


def later_kernel(jobs, rows_ref, labs_ref, vals_ref, x_ref, *refs):
    out_refs, acc_ref = refs[: len(jobs)], refs[len(jobs)]
    for (other, steps), out_ref in zip(jobs, out_refs):
        product(other, steps, rows_ref, labs_ref, vals_ref, x_ref, out_ref, acc_ref)


def route_kernel(ids_ref, place_ref, inside_ref):
    slots, owners, labs = place_ref.shape
    ids = ids_ref[...]
    down = lax.broadcasted_iota(jnp.int32, (labs, labs), 0)
    across = lax.broadcasted_iota(jnp.int32, (labs, labs), 1)
    ids_down = jnp.sum(jnp.where(down == across, ids, 0), axis=1, keepdims=True)
    owner = ids // CL_OWN
    earlier = (ids_down // CL_OWN == owner) & (down < across)
    rank = jnp.sum(earlier.astype(jnp.int32), axis=0, keepdims=True)
    here = lax.broadcasted_iota(jnp.int32, (owners, labs), 0) == owner
    for slot in range(slots):
        place_ref[slot] = jnp.where(here & (rank == slot), 1.0, 0.0).astype(BF)
    inside_ref[...] = jnp.broadcast_to((ids_down % CL_OWN).astype(F32), inside_ref.shape).astype(BF)


def load_kernel(own_ref, mate_ref, far_ref, out_ref):
    out_ref[...] = (own_ref[...].astype(F32) + mate_ref[...].astype(F32) + far_ref[...].astype(F32)).astype(BF)


def pack_kernel(most_ref, came_ref, place_ref, inside_ref, emb_ref, out_ref, stage_ref):
    width = emb_ref.shape[1]
    slots, owners = place_ref.shape[:2]
    cols = width // LANES
    step = (cols + 1) * slots
    summed = most_ref[...] + came_ref[...].astype(F32)
    unit = summed * lax.rsqrt(jnp.sum(summed * summed, axis=-1, keepdims=True) + 1e-06)
    emb_ref[...] = unit
    unit = unit.astype(BF)
    for slot in range(slots):
        moved = jnp.dot(place_ref[slot], unit, preferred_element_type=F32)
        for col in range(cols):
            stage_ref[pl.ds(col * slots + slot, owners, stride=step), :] = moved[:, col * LANES : (col + 1) * LANES]
        stage_ref[pl.ds(cols * slots + slot, owners, stride=step), :] = jnp.dot(
            place_ref[slot], inside_ref[...], preferred_element_type=F32
        )
    out_ref.reshape(owners * step, LANES)[...] = stage_ref[...].astype(BF)


def combine_kernel(got_ref, out_ref, stage_ref):
    owners, cols = got_ref.shape[0], got_ref.shape[1] - 1
    step = (cols + 1) * SLOTS
    stage_ref[...] = got_ref.reshape(owners * step, LANES)[...].astype(F32)
    lane = lax.broadcasted_iota(jnp.int32, (owners, LANES), 1).astype(F32)
    total = jnp.zeros((LANES, cols * LANES), F32)
    for slot in range(SLOTS):
        inside = stage_ref[pl.ds(cols * SLOTS + slot, owners, stride=step), :]
        member = jnp.where(inside == lane, 1.0, 0.0).astype(BF)
        rows = jnp.concatenate(
            [stage_ref[pl.ds(col * SLOTS + slot, owners, stride=step), :].astype(BF) for col in range(cols)], axis=1
        )
        total = total + lax.dot_general(member, rows, (((0,), (0,)), ((), ())), preferred_element_type=F32)
    sums = total[:CL_OWN]
    out_ref[...] = sums * lax.rsqrt(jnp.sum(sums * sums, axis=-1, keepdims=True) + 1e-06)


def shards(features, tile_rows, tile_labels, tile_values, cluster_ids):
    tiles, tile = tile_values.shape[:2]
    insts, width = features.shape
    labs = cluster_ids.shape[0]
    chips = lax.axis_size("x")
    owners = lax.axis_size(INST + LAB)
    cols = width // LANES
    smem = pl.BlockSpec(memory_space=pltpu.MemorySpace.SMEM)
    hbm = pl.BlockSpec(memory_space=pltpu.MemorySpace.HBM)
    tile_scratch = [pltpu.SMEM((tiles,), jnp.int32)] * 2 + [pltpu.VMEM(tile_values.shape, BF)]
    far_steps, near_steps = (2,), (0, 1, -1)

    def product_cost(steps):
        return pl.CostEstimate(
            flops=len(steps) * tile * tile * width * 2,
            bytes_accessed=2 * (tiles * tile * tile + insts * width + len(steps) * tile * width),
            transcendentals=0,
        )

    far_away, normed = pl.pallas_call(
        functools.partial(first_kernel, far_steps),
        grid=(1,),
        out_shape=(jax.ShapeDtypeStruct((tile, width), BF), jax.ShapeDtypeStruct((insts, width), BF)),
        in_specs=[hbm] * 4,
        out_specs=(full((tile, width)), full((insts, width))),
        scratch_shapes=tile_scratch
        + [pltpu.VMEM((insts, width), BF), pltpu.VMEM((tile, width), F32), pltpu.SemaphoreType.DMA((4,))],
        compiler_params=params(),
        cost_estimate=product_cost(far_steps),
        name="far_away",
    )(*(in_hbm(a) for a in (tile_rows, tile_labels, tile_values, features)))

    def later(name, x, *jobs):
        shapes = [(len(steps) * tile, width) for _, steps in jobs]
        return pl.pallas_call(
            functools.partial(later_kernel, jobs),
            grid=(1,),
            out_shape=[jax.ShapeDtypeStruct(shape, BF) for shape in shapes],
            in_specs=[smem] * 2 + [full(tile_values.shape), full((insts, width))],
            out_specs=[full(shape) for shape in shapes],
            scratch_shapes=[pltpu.VMEM((tile, width), F32)],
            compiler_params=params(),
            cost_estimate=product_cost(sum((steps for _, steps in jobs), ())),
            name=name,
        )(tile_rows, tile_labels, tile_values, x)

    def across(block):
        return lax.ppermute(block, "c", [(0, 1), (1, 0)])

    def along(block, step):
        pairs = [(i, i + step * (1 - 2 * c)) for i in range(chips) for c in range(CORES)]
        pairs = [(i * CORES + k % CORES, j % chips * CORES + k % CORES) for k, (i, j) in enumerate(pairs)]
        return lax.ppermute(block, INST, pairs)

    far_mate = across(far_away)
    far_own, near_away = later("far_own", normed, (False, far_steps), (True, near_steps))
    far = (far_own.astype(F32) + far_mate.astype(F32)).astype(BF)
    ids, normed, near_away, far = lax.optimization_barrier((cluster_ids, normed, near_away, far))
    far_came = along(far, 1)
    mate = across(near_away)
    (own,) = later("near_own", normed, (False, near_steps))

    def pair(k):
        return own[k * tile : (k + 1) * tile].astype(F32) + mate[k * tile : (k + 1) * tile].astype(F32)

    free_came = along(pair(2).astype(BF), -1)
    block = full((tile, width))
    loaded = pl.pallas_call(
        load_kernel,
        grid=(1,),
        out_shape=jax.ShapeDtypeStruct((tile, width), BF),
        in_specs=[pl.BlockSpec((tile, width), lambda *_: (1, 0))] * 2 + [block],
        out_specs=block,
        compiler_params=params(),
        name="load",
    )(own, mate, far_came)
    came = along(loaded, 1)
    most = pair(0) + free_came.astype(F32)
    place, inside = pl.pallas_call(
        route_kernel,
        grid=(1,),
        out_shape=(jax.ShapeDtypeStruct((SLOTS, owners, labs), BF), jax.ShapeDtypeStruct((labs, LANES), BF)),
        in_specs=[full((1, labs))],
        out_specs=(full((SLOTS, owners, labs)), full((labs, LANES))),
        compiler_params=params(),
        name="route",
    )(ids.reshape(1, labs))
    block = full((tile, width))
    message = (owners, cols + 1, SLOTS, LANES)
    stage = pltpu.VMEM((owners * (cols + 1) * SLOTS, LANES), F32)
    label_embed, rows = pl.pallas_call(
        pack_kernel,
        grid=(1,),
        out_shape=(jax.ShapeDtypeStruct((labs, width), F32), jax.ShapeDtypeStruct(message, BF)),
        in_specs=[block] * 2 + [full((SLOTS, owners, labs)), full((labs, LANES))],
        out_specs=(full((labs, width)), full(message)),
        scratch_shapes=[stage],
        compiler_params=params(),
        name="pack",
    )(most, came, place, inside)
    got = lax.all_to_all(rows, INST + LAB, 0, 0, tiled=True)
    centroids = pl.pallas_call(
        combine_kernel,
        grid=(1,),
        out_shape=jax.ShapeDtypeStruct((CL_OWN, width), F32),
        in_specs=[full(message)],
        out_specs=full((CL_OWN, width)),
        scratch_shapes=[stage],
        compiler_params=params(),
        name="combine",
    )(got)
    return label_embed, centroids


def solution(mesh):
    insts, labs = mesh.devices.shape
    cut = (insts // CORES, CORES, labs // Y_CHIPS, Y_CHIPS)
    return jax.shard_map(
        shards,
        mesh=Mesh(mesh.devices.reshape(cut), INST + LAB),
        in_specs=(P(INST, None), P(INST + LAB), P(INST + LAB), P(INST + LAB, None, None), P(LAB + INST)),
        out_specs=(P(LAB + INST, None), P(INST + LAB, None)),
        check_vma=False,
    )
```

```python
import functools

import jax
import jax.numpy as jnp
from jax import lax
from jax.experimental import pallas as pl
from jax.experimental.pallas import tpu as pltpu
from jax.sharding import Mesh
from jax.sharding import PartitionSpec as P

CL_OWN = 32
RT = 2
SLOTS = 2
LANES = 128
CORES = 2
Y_CHIPS = 4
INST = ("x", "c")
LAB = ("z", "y")
BF = jnp.bfloat16
F32 = jnp.float32


def full(shape):
    return pl.BlockSpec(shape, lambda *_: (0,) * len(shape))


def params(**kwargs):
    return pltpu.CompilerParams(vmem_limit_bytes=24 << 20, **kwargs)


def in_hbm(array):
    return pltpu.with_memory_space_constraint(array, pltpu.MemorySpace.HBM)


def tiles_in(rows_hbm, labs_hbm, vals_hbm, rows_ref, labs_ref, vals_ref, sems):
    pairs = ((rows_hbm, rows_ref), (labs_hbm, labs_ref), (vals_hbm, vals_ref))
    return [pltpu.make_async_copy(src, dst, sems.at[k]) for k, (src, dst) in enumerate(pairs)]


def times(values, x):
    return lax.dot_general(values, x, (((0,), (0,)), ((), ())), preferred_element_type=F32)


def product(other, steps, rows_ref, labs_ref, vals_ref, x_ref, out_ref):
    tiles, tile = vals_ref.shape[0], vals_ref.shape[1]
    chips = lax.axis_size("x")
    core = lax.axis_index("c")
    if other:
        core = 1 - core
    for k, step in enumerate(steps):
        lab = lax.rem(lax.axis_index("x") + step * (1 - 2 * core) + chips, chips) * CORES + core
        held = []
        for r in range(RT):
            n = jnp.int32(-1)
            for t in range(tiles):
                n = jnp.where((rows_ref[t] == r) & (labs_ref[t] == lab), t, n)
            held.append(n)
        top, low = held
        count = (top >= 0).astype(jnp.int32) + (low >= 0).astype(jnp.int32)
        one = jnp.maximum(top, low)
        where = jnp.where(top >= 0, 0, tile)
        spot = pl.ds(k * tile, tile)

        @pl.when(count == 0)
        def _(spot=spot):
            out_ref[spot, :] = jnp.zeros((tile, out_ref.shape[1]), BF)

        @pl.when(count == 1)
        def _(spot=spot, one=one, where=where):
            out_ref[spot, :] = times(vals_ref[one], x_ref[pl.ds(pl.multiple_of(where, tile), tile), :]).astype(BF)

        @pl.when(count == 2)
        def _(spot=spot, top=top, low=low):
            both = times(vals_ref[top], x_ref[:tile, :]) + times(vals_ref[low], x_ref[tile:, :])
            out_ref[spot, :] = both.astype(BF)


def first_kernel(
    steps, rows_hbm, labs_hbm, vals_hbm, feat_hbm, out_ref, x_ref, rows_ref, labs_ref, vals_ref, feat_ref, sems
):
    feat_in = pltpu.make_async_copy(feat_hbm, feat_ref, sems.at[3])
    copies = tiles_in(rows_hbm, labs_hbm, vals_hbm, rows_ref, labs_ref, vals_ref, sems)
    feat_in.start()
    for copy in copies:
        copy.start()
    feat_in.wait()
    f = feat_ref[...].astype(F32)
    x_ref[...] = (f * lax.rsqrt(jnp.sum(f * f, axis=-1, keepdims=True) + 1e-06)).astype(BF)
    for copy in copies:
        copy.wait()
    product(True, steps, rows_ref, labs_ref, vals_ref, x_ref, out_ref)


def later_kernel(jobs, rows_ref, labs_ref, vals_ref, x_ref, *out_refs):
    for (other, steps), out_ref in zip(jobs, out_refs):
        product(other, steps, rows_ref, labs_ref, vals_ref, x_ref, out_ref)


def route_kernel(ids_ref, place_ref, inside_ref):
    rows, labs = place_ref.shape
    ids = ids_ref[...]
    down = lax.broadcasted_iota(jnp.int32, (labs, labs), 0)
    across = lax.broadcasted_iota(jnp.int32, (labs, labs), 1)
    ids_down = jnp.sum(jnp.where(down == across, ids, 0), axis=1, keepdims=True)
    owner = ids // CL_OWN
    earlier = (ids_down // CL_OWN == owner) & (down < across)
    row = owner * SLOTS + jnp.sum(earlier.astype(jnp.int32), axis=0, keepdims=True)
    place_ref[...] = jnp.where(lax.broadcasted_iota(jnp.int32, (rows, labs), 0) == row, 1.0, 0.0).astype(BF)
    inside_ref[...] = jnp.broadcast_to((ids_down % CL_OWN).astype(F32), inside_ref.shape).astype(BF)


def load_kernel(own_ref, mate_ref, far_ref, out_ref):
    out_ref[...] = (own_ref[...].astype(F32) + mate_ref[...].astype(F32) + far_ref[...].astype(F32)).astype(BF)


def pack_kernel(most_ref, came_ref, place_ref, inside_ref, emb_hbm, out_ref, emb_ref, sem):
    owners, cols = out_ref.shape[0], out_ref.shape[1] - 1
    summed = most_ref[...] + came_ref[...].astype(F32)
    unit = summed * lax.rsqrt(jnp.sum(summed * summed, axis=-1, keepdims=True) + 1e-06)
    emb_ref[...] = unit
    emb_out = pltpu.make_async_copy(emb_ref, emb_hbm, sem)
    emb_out.start()
    place = place_ref[...]
    moved = jnp.dot(place, unit.astype(BF), preferred_element_type=F32).astype(BF)
    for col in range(cols):
        out_ref[:, col] = moved[:, col * LANES : (col + 1) * LANES].reshape(owners, SLOTS, LANES)
    inside = jnp.dot(place, inside_ref[...], preferred_element_type=F32).astype(BF)
    out_ref[:, cols] = inside.reshape(owners, SLOTS, LANES)
    emb_out.wait()


def combine_kernel(got_ref, out_ref):
    owners, cols = got_ref.shape[0], got_ref.shape[1] - 1
    rows = owners * SLOTS
    inside = got_ref[:, cols].reshape(rows, LANES).astype(F32)
    lane = lax.broadcasted_iota(jnp.int32, (rows, LANES), 1).astype(F32)
    member = jnp.where(inside == lane, 1.0, 0.0).astype(BF)
    data = jnp.concatenate([got_ref[:, col].reshape(rows, LANES) for col in range(cols)], axis=1)
    sums = lax.dot_general(member, data, (((0,), (0,)), ((), ())), preferred_element_type=F32)[:CL_OWN]
    out_ref[...] = sums * lax.rsqrt(jnp.sum(sums * sums, axis=-1, keepdims=True) + 1e-06)


def shards(features, tile_rows, tile_labels, tile_values, cluster_ids):
    tiles, tile = tile_values.shape[:2]
    insts, width = features.shape
    labs = cluster_ids.shape[0]
    chips = lax.axis_size("x")
    owners = lax.axis_size(INST + LAB)
    cols = width // LANES
    smem = pl.BlockSpec(memory_space=pltpu.MemorySpace.SMEM)
    hbm = pl.BlockSpec(memory_space=pltpu.MemorySpace.HBM)
    tile_scratch = [pltpu.SMEM((tiles,), jnp.int32)] * 2 + [pltpu.VMEM(tile_values.shape, BF)]
    far_steps, near_steps = (2,), (0, 1, -1)

    def product_cost(steps):
        return pl.CostEstimate(
            flops=len(steps) * tile * tile * width * 2,
            bytes_accessed=2 * (tiles * tile * tile + insts * width + len(steps) * tile * width),
            transcendentals=0,
        )

    far_away, normed = pl.pallas_call(
        functools.partial(first_kernel, far_steps),
        grid=(1,),
        out_shape=(jax.ShapeDtypeStruct((tile, width), BF), jax.ShapeDtypeStruct((insts, width), BF)),
        in_specs=[hbm] * 4,
        out_specs=(full((tile, width)), full((insts, width))),
        scratch_shapes=tile_scratch
        + [pltpu.VMEM((insts, width), BF), pltpu.SemaphoreType.DMA((4,))],
        compiler_params=params(),
        cost_estimate=product_cost(far_steps),
        name="far_away",
    )(*(in_hbm(a) for a in (tile_rows, tile_labels, tile_values, features)))

    def later(name, x, *jobs):
        shapes = [(len(steps) * tile, width) for _, steps in jobs]
        return pl.pallas_call(
            functools.partial(later_kernel, jobs),
            grid=(1,),
            out_shape=[jax.ShapeDtypeStruct(shape, BF) for shape in shapes],
            in_specs=[smem] * 2 + [full(tile_values.shape), full((insts, width))],
            out_specs=[full(shape) for shape in shapes],
            compiler_params=params(),
            cost_estimate=product_cost(sum((steps for _, steps in jobs), ())),
            name=name,
        )(tile_rows, tile_labels, tile_values, x)

    def across(block):
        return lax.ppermute(block, "c", [(0, 1), (1, 0)])

    def along(block, step):
        pairs = [(i, i + step * (1 - 2 * c)) for i in range(chips) for c in range(CORES)]
        pairs = [(i * CORES + k % CORES, j % chips * CORES + k % CORES) for k, (i, j) in enumerate(pairs)]
        return lax.ppermute(block, INST, pairs)

    far_mate = across(far_away)
    far_own, near_away = later("far_own", normed, (False, far_steps), (True, near_steps))
    far = (far_own.astype(F32) + far_mate.astype(F32)).astype(BF)
    ids, normed, near_away, far = lax.optimization_barrier((cluster_ids, normed, near_away, far))
    far_came = along(far, 1)
    mate = across(near_away)
    (own,) = later("near_own", normed, (False, near_steps))

    def pair(k):
        return own[k * tile : (k + 1) * tile].astype(F32) + mate[k * tile : (k + 1) * tile].astype(F32)

    free_came = along(pair(2).astype(BF), -1)
    block = full((tile, width))
    loaded = pl.pallas_call(
        load_kernel,
        grid=(1,),
        out_shape=jax.ShapeDtypeStruct((tile, width), BF),
        in_specs=[pl.BlockSpec((tile, width), lambda *_: (1, 0))] * 2 + [block],
        out_specs=block,
        compiler_params=params(),
        name="load",
    )(own, mate, far_came)
    came = along(loaded, 1)
    most = pair(0) + free_came.astype(F32)
    place, inside = pl.pallas_call(
        route_kernel,
        grid=(1,),
        out_shape=(jax.ShapeDtypeStruct((SLOTS * owners, labs), BF), jax.ShapeDtypeStruct((labs, LANES), BF)),
        in_specs=[full((1, labs))],
        out_specs=(full((SLOTS * owners, labs)), full((labs, LANES))),
        compiler_params=params(),
        name="route",
    )(ids.reshape(1, labs))
    block = full((tile, width))
    message = (owners, cols + 1, SLOTS, LANES)
    label_embed, rows = pl.pallas_call(
        pack_kernel,
        grid=(1,),
        out_shape=(jax.ShapeDtypeStruct((labs, width), F32), jax.ShapeDtypeStruct(message, BF)),
        in_specs=[block] * 2 + [full((SLOTS * owners, labs)), full((labs, LANES))],
        out_specs=(hbm, full(message)),
        scratch_shapes=[pltpu.VMEM((labs, width), F32), pltpu.SemaphoreType.DMA],
        compiler_params=params(),
        name="pack",
    )(most, came, place, inside)
    got = lax.all_to_all(rows, INST + LAB, 0, 0, tiled=True)
    centroids = pl.pallas_call(
        combine_kernel,
        grid=(1,),
        out_shape=jax.ShapeDtypeStruct((CL_OWN, width), F32),
        in_specs=[full(message)],
        out_specs=full((CL_OWN, width)),
        compiler_params=params(),
        name="combine",
    )(got)
    return label_embed, centroids


def solution(mesh):
    insts, labs = mesh.devices.shape
    cut = (insts // CORES, CORES, labs // Y_CHIPS, Y_CHIPS)
    return jax.shard_map(
        shards,
        mesh=Mesh(mesh.devices.reshape(cut), INST + LAB),
        in_specs=(P(INST, None), P(INST + LAB), P(INST + LAB), P(INST + LAB, None, None), P(LAB + INST)),
        out_specs=(P(LAB + INST, None), P(INST + LAB, None)),
        check_vma=False,
    )
```

```python
import functools

import jax
import jax.numpy as jnp
from jax import lax
from jax.experimental import pallas as pl
from jax.experimental.pallas import tpu as pltpu
from jax.sharding import Mesh
from jax.sharding import PartitionSpec as P

CL_OWN = 32
RT = 2
SLOTS = 2
LANES = 128
CORES = 2
Y_CHIPS = 4
INST = ("x", "c")
LAB = ("z", "y")
BF = jnp.bfloat16
F32 = jnp.float32


def full(shape):
    return pl.BlockSpec(shape, lambda *_: (0,) * len(shape))


def params(**kwargs):
    return pltpu.CompilerParams(vmem_limit_bytes=24 << 20, **kwargs)


def in_hbm(array):
    return pltpu.with_memory_space_constraint(array, pltpu.MemorySpace.HBM)


def times(values, x):
    return lax.dot_general(values, x, (((0,), (0,)), ((), ())), preferred_element_type=F32)


def tiles_of(other, step, rows_ref, labs_ref):
    chips = lax.axis_size("x")
    core = lax.axis_index("c")
    if other:
        core = 1 - core
    lab = lax.rem(lax.axis_index("x") + step * (1 - 2 * core) + chips, chips) * CORES + core
    held = []
    for r in range(RT):
        n = jnp.int32(-1)
        for t in range(rows_ref.shape[0]):
            n = jnp.where((rows_ref[t] == r) & (labs_ref[t] == lab), t, n)
        held.append(n)
    return held


def product(top, low, pick, x_ref, out_ref, spot):
    tile = x_ref.shape[0] // RT

    @pl.when((top < 0) & (low < 0))
    def _():
        out_ref[spot, :] = jnp.zeros((tile, out_ref.shape[1]), BF)

    @pl.when((top >= 0) & (low < 0))
    def _():
        out_ref[spot, :] = times(pick(top, 0), x_ref[:tile, :]).astype(BF)

    @pl.when((top < 0) & (low >= 0))
    def _():
        out_ref[spot, :] = times(pick(low, 1), x_ref[tile:, :]).astype(BF)

    @pl.when((top >= 0) & (low >= 0))
    def _():
        out_ref[spot, :] = (times(pick(top, 0), x_ref[:tile, :]) + times(pick(low, 1), x_ref[tile:, :])).astype(BF)


def first_kernel(step, rows_hbm, labs_hbm, vals_hbm, feat_hbm, out_ref, x_ref, rows_ref, labs_ref, two_ref, feat_ref, sems):
    tile = two_ref.shape[1]
    halves = [slice(r * tile, (r + 1) * tile) for r in range(RT)]
    lists = [
        pltpu.make_async_copy(rows_hbm, rows_ref, sems.at[0]),
        pltpu.make_async_copy(labs_hbm, labs_ref, sems.at[1]),
    ]
    feats = [pltpu.make_async_copy(feat_hbm.at[h], feat_ref.at[h], sems.at[2 + r]) for r, h in enumerate(halves)]
    for copy in lists + feats:
        copy.start()
    for copy in lists:
        copy.wait()
    held = tiles_of(True, step, rows_ref, labs_ref)
    tiles = [
        pltpu.make_async_copy(vals_hbm.at[jnp.maximum(n, 0)], two_ref.at[r], sems.at[2 + RT + r])
        for r, n in enumerate(held)
    ]
    for copy in tiles:
        copy.start()
    for copy, h in zip(feats, halves):
        copy.wait()
        f = feat_ref[h, :].astype(F32)
        x_ref[h, :] = (f * lax.rsqrt(jnp.sum(f * f, axis=-1, keepdims=True) + 1e-06)).astype(BF)
    for copy in tiles:
        copy.wait()
    product(*held, lambda n, r: two_ref[r], x_ref, out_ref, slice(0, tile))


def later_kernel(jobs, rows_ref, labs_ref, vals_ref, x_ref, *out_refs):
    tile = vals_ref.shape[1]
    for (other, steps), out_ref in zip(jobs, out_refs):
        for k, step in enumerate(steps):
            held = tiles_of(other, step, rows_ref, labs_ref)
            product(*held, lambda n, r: vals_ref[n], x_ref, out_ref, slice(k * tile, (k + 1) * tile))


def route_kernel(ids_ref, place_ref, inside_ref):
    rows, labs = place_ref.shape
    ids = ids_ref[...]
    down = lax.broadcasted_iota(jnp.int32, (labs, labs), 0)
    across = lax.broadcasted_iota(jnp.int32, (labs, labs), 1)
    ids_down = jnp.sum(jnp.where(down == across, ids, 0), axis=1, keepdims=True)
    owner = ids // CL_OWN
    earlier = (ids_down // CL_OWN == owner) & (down < across)
    row = owner * SLOTS + jnp.sum(earlier.astype(jnp.int32), axis=0, keepdims=True)
    place_ref[...] = jnp.where(lax.broadcasted_iota(jnp.int32, (rows, labs), 0) == row, 1.0, 0.0).astype(BF)
    inside_ref[...] = jnp.broadcast_to((ids_down % CL_OWN).astype(F32), inside_ref.shape).astype(BF)


def load_kernel(own_ref, mate_ref, far_ref, out_ref):
    out_ref[...] = (own_ref[...].astype(F32) + mate_ref[...].astype(F32) + far_ref[...].astype(F32)).astype(BF)


def pack_kernel(most_ref, came_ref, place_ref, inside_ref, emb_ref, out_ref):
    owners, cols = out_ref.shape[0], out_ref.shape[1] - 1
    summed = most_ref[...] + came_ref[...].astype(F32)
    unit = summed * lax.rsqrt(jnp.sum(summed * summed, axis=-1, keepdims=True) + 1e-06)
    emb_ref[...] = unit
    place = place_ref[...]
    moved = jnp.dot(place, unit.astype(BF), preferred_element_type=F32).astype(BF)
    for col in range(cols):
        out_ref[:, col] = moved[:, col * LANES : (col + 1) * LANES].reshape(owners, SLOTS, LANES)
    inside = jnp.dot(place, inside_ref[...], preferred_element_type=F32).astype(BF)
    out_ref[:, cols] = inside.reshape(owners, SLOTS, LANES)


def combine_kernel(got_ref, emb_ref, out_ref, emb_hbm, sem):
    emb_out = pltpu.make_async_copy(emb_ref, emb_hbm, sem)
    emb_out.start()
    owners, cols = got_ref.shape[0], got_ref.shape[1] - 1
    rows = owners * SLOTS
    inside = got_ref[:, cols].reshape(rows, LANES).astype(F32)
    lane = lax.broadcasted_iota(jnp.int32, (rows, LANES), 1).astype(F32)
    member = jnp.where(inside == lane, 1.0, 0.0).astype(BF)
    data = jnp.concatenate([got_ref[:, col].reshape(rows, LANES) for col in range(cols)], axis=1)
    sums = lax.dot_general(member, data, (((0,), (0,)), ((), ())), preferred_element_type=F32)[:CL_OWN]
    out_ref[...] = sums * lax.rsqrt(jnp.sum(sums * sums, axis=-1, keepdims=True) + 1e-06)
    emb_out.wait()


def shards(features, tile_rows, tile_labels, tile_values, cluster_ids):
    tiles, tile = tile_values.shape[:2]
    insts, width = features.shape
    labs = cluster_ids.shape[0]
    chips = lax.axis_size("x")
    owners = lax.axis_size(INST + LAB)
    cols = width // LANES
    smem = pl.BlockSpec(memory_space=pltpu.MemorySpace.SMEM)
    hbm = pl.BlockSpec(memory_space=pltpu.MemorySpace.HBM)
    far_steps, near_steps = (2,), (0, 1, -1)

    def product_cost(steps):
        return pl.CostEstimate(
            flops=len(steps) * tile * tile * width * 2,
            bytes_accessed=2 * (tiles * tile * tile + insts * width + len(steps) * tile * width),
            transcendentals=0,
        )

    far_away, normed = pl.pallas_call(
        functools.partial(first_kernel, *far_steps),
        grid=(1,),
        out_shape=(jax.ShapeDtypeStruct((tile, width), BF), jax.ShapeDtypeStruct((insts, width), BF)),
        in_specs=[hbm] * 4,
        out_specs=(full((tile, width)), full((insts, width))),
        scratch_shapes=[
            pltpu.SMEM((tiles,), jnp.int32),
            pltpu.SMEM((tiles,), jnp.int32),
            pltpu.VMEM((RT, tile, tile), BF),
            pltpu.VMEM((insts, width), BF),
            pltpu.SemaphoreType.DMA((2 + 2 * RT,)),
        ],
        compiler_params=params(),
        cost_estimate=product_cost(far_steps),
        name="far_away",
    )(*(in_hbm(a) for a in (tile_rows, tile_labels, tile_values, features)))

    def later(name, x, *jobs):
        shapes = [(len(steps) * tile, width) for _, steps in jobs]
        return pl.pallas_call(
            functools.partial(later_kernel, jobs),
            grid=(1,),
            out_shape=[jax.ShapeDtypeStruct(shape, BF) for shape in shapes],
            in_specs=[smem] * 2 + [full(tile_values.shape), full((insts, width))],
            out_specs=[full(shape) for shape in shapes],
            compiler_params=params(),
            cost_estimate=product_cost(sum((steps for _, steps in jobs), ())),
            name=name,
        )(tile_rows, tile_labels, tile_values, x)

    def across(block):
        return lax.ppermute(block, "c", [(0, 1), (1, 0)])

    def along(block, step):
        pairs = [(i, i + step * (1 - 2 * c)) for i in range(chips) for c in range(CORES)]
        pairs = [(i * CORES + k % CORES, j % chips * CORES + k % CORES) for k, (i, j) in enumerate(pairs)]
        return lax.ppermute(block, INST, pairs)

    far_mate = across(far_away)
    far_own, near_away = later("far_own", normed, (False, far_steps), (True, near_steps))
    far = (far_own.astype(F32) + far_mate.astype(F32)).astype(BF)
    ids, normed, near_away, far = lax.optimization_barrier((cluster_ids, normed, near_away, far))
    far_came = along(far, 1)
    mate = across(near_away)
    (own,) = later("near_own", normed, (False, near_steps))

    def pair(k):
        return own[k * tile : (k + 1) * tile].astype(F32) + mate[k * tile : (k + 1) * tile].astype(F32)

    free_came = along(pair(2).astype(BF), -1)
    block = full((tile, width))
    loaded = pl.pallas_call(
        load_kernel,
        grid=(1,),
        out_shape=jax.ShapeDtypeStruct((tile, width), BF),
        in_specs=[pl.BlockSpec((tile, width), lambda *_: (1, 0))] * 2 + [block],
        out_specs=block,
        compiler_params=params(),
        name="load",
    )(own, mate, far_came)
    came = along(loaded, 1)
    most = pair(0) + free_came.astype(F32)
    place, inside = pl.pallas_call(
        route_kernel,
        grid=(1,),
        out_shape=(jax.ShapeDtypeStruct((SLOTS * owners, labs), BF), jax.ShapeDtypeStruct((labs, LANES), BF)),
        in_specs=[full((1, labs))],
        out_specs=(full((SLOTS * owners, labs)), full((labs, LANES))),
        compiler_params=params(),
        name="route",
    )(ids.reshape(1, labs))
    block = full((tile, width))
    message = (owners, cols + 1, SLOTS, LANES)
    embed = jax.ShapeDtypeStruct((labs, width), F32)
    unit, rows = pl.pallas_call(
        pack_kernel,
        grid=(1,),
        out_shape=(embed, jax.ShapeDtypeStruct(message, BF)),
        in_specs=[block] * 2 + [full((SLOTS * owners, labs)), full((labs, LANES))],
        out_specs=(full((labs, width)), full(message)),
        compiler_params=params(),
        name="pack",
    )(most, came, place, inside)
    got = lax.all_to_all(rows, INST + LAB, 0, 0, tiled=True)
    centroids, label_embed = pl.pallas_call(
        combine_kernel,
        grid=(1,),
        out_shape=(jax.ShapeDtypeStruct((CL_OWN, width), F32), embed),
        in_specs=[full(message), full((labs, width))],
        out_specs=(full((CL_OWN, width)), hbm),
        scratch_shapes=[pltpu.SemaphoreType.DMA],
        compiler_params=params(),
        name="combine",
    )(got, unit)
    return label_embed, centroids


def solution(mesh):
    insts, labs = mesh.devices.shape
    cut = (insts // CORES, CORES, labs // Y_CHIPS, Y_CHIPS)
    return jax.shard_map(
        shards,
        mesh=Mesh(mesh.devices.reshape(cut), INST + LAB),
        in_specs=(P(INST, None), P(INST + LAB), P(INST + LAB), P(INST + LAB, None, None), P(LAB + INST)),
        out_specs=(P(LAB + INST, None), P(INST + LAB, None)),
        check_vma=False,
    )
```

```python
import functools

import jax
import jax.numpy as jnp
from jax import lax
from jax.experimental import pallas as pl
from jax.experimental.pallas import tpu as pltpu
from jax.sharding import Mesh
from jax.sharding import PartitionSpec as P

CL_OWN = 32
RT = 2
SLOTS = 2
LANES = 128
CORES = 2
Y_CHIPS = 4
INST = ("x", "c")
LAB = ("z", "y")
BF = jnp.bfloat16
F32 = jnp.float32


def full(shape):
    return pl.BlockSpec(shape, lambda *_: (0,) * len(shape))


def params(**kwargs):
    return pltpu.CompilerParams(vmem_limit_bytes=24 << 20, **kwargs)


def in_hbm(array):
    return pltpu.with_memory_space_constraint(array, pltpu.MemorySpace.HBM)


def tiles_in(rows_hbm, labs_hbm, vals_hbm, rows_ref, labs_ref, vals_ref, sems):
    pairs = ((rows_hbm, rows_ref), (labs_hbm, labs_ref), (vals_hbm, vals_ref))
    return [pltpu.make_async_copy(src, dst, sems.at[k]) for k, (src, dst) in enumerate(pairs)]


def times(values, x):
    return lax.dot_general(values, x, (((0,), (0,)), ((), ())), preferred_element_type=F32)


def product(other, steps, rows_ref, labs_ref, vals_ref, x_ref, out_ref):
    tiles, tile = vals_ref.shape[0], vals_ref.shape[1]
    chips = lax.axis_size("x")
    core = lax.axis_index("c")
    if other:
        core = 1 - core
    for k, step in enumerate(steps):
        lab = lax.rem(lax.axis_index("x") + step * (1 - 2 * core) + chips, chips) * CORES + core
        held = []
        for r in range(RT):
            n = jnp.int32(-1)
            for t in range(tiles):
                n = jnp.where((rows_ref[t] == r) & (labs_ref[t] == lab), t, n)
            held.append(n)
        top, low = held
        count = (top >= 0).astype(jnp.int32) + (low >= 0).astype(jnp.int32)
        one = jnp.maximum(top, low)
        where = jnp.where(top >= 0, 0, tile)
        spot = pl.ds(k * tile, tile)

        @pl.when(count == 0)
        def _(spot=spot):
            out_ref[spot, :] = jnp.zeros((tile, out_ref.shape[1]), BF)

        @pl.when(count == 1)
        def _(spot=spot, one=one, where=where):
            out_ref[spot, :] = times(vals_ref[one], x_ref[pl.ds(pl.multiple_of(where, tile), tile), :]).astype(BF)

        @pl.when(count == 2)
        def _(spot=spot, top=top, low=low):
            both = times(vals_ref[top], x_ref[:tile, :]) + times(vals_ref[low], x_ref[tile:, :])
            out_ref[spot, :] = both.astype(BF)


def first_kernel(
    steps, rows_hbm, labs_hbm, vals_hbm, feat_hbm, out_ref, x_ref, rows_ref, labs_ref, vals_ref, feat_ref, sems
):
    feat_in = pltpu.make_async_copy(feat_hbm, feat_ref, sems.at[3])
    copies = tiles_in(rows_hbm, labs_hbm, vals_hbm, rows_ref, labs_ref, vals_ref, sems)
    feat_in.start()
    for copy in copies:
        copy.start()
    feat_in.wait()
    f = feat_ref[...].astype(F32)
    x_ref[...] = (f * lax.rsqrt(jnp.sum(f * f, axis=-1, keepdims=True) + 1e-06)).astype(BF)
    for copy in copies:
        copy.wait()
    product(True, steps, rows_ref, labs_ref, vals_ref, x_ref, out_ref)


def later_kernel(jobs, rows_ref, labs_ref, vals_ref, x_ref, *out_refs):
    for (other, steps), out_ref in zip(jobs, out_refs):
        product(other, steps, rows_ref, labs_ref, vals_ref, x_ref, out_ref)


def route_kernel(n_lab, ids_ref, place_ref, inside_ref):
    rows, labs = place_ref.shape
    ids = ids_ref[...]
    down = lax.broadcasted_iota(jnp.int32, (labs, labs), 0)
    across = lax.broadcasted_iota(jnp.int32, (labs, labs), 1)
    ids_down = jnp.sum(jnp.where(down == across, ids, 0), axis=1, keepdims=True)
    owner = ids // CL_OWN
    earlier = (ids_down // CL_OWN == owner) & (down < across)
    rank = jnp.sum(earlier.astype(jnp.int32), axis=0, keepdims=True)
    core = owner // n_lab % CORES
    chip = owner // (n_lab * CORES) * n_lab + owner % n_lab
    row = core * (rows // CORES) + chip * SLOTS + rank
    place_ref[...] = jnp.where(lax.broadcasted_iota(jnp.int32, (rows, labs), 0) == row, 1.0, 0.0).astype(BF)
    inside_ref[...] = jnp.broadcast_to((ids_down % CL_OWN).astype(F32), inside_ref.shape).astype(BF)


def load_kernel(own_ref, mate_ref, far_ref, out_ref):
    out_ref[...] = (own_ref[...].astype(F32) + mate_ref[...].astype(F32) + far_ref[...].astype(F32)).astype(BF)


def pack_kernel(most_ref, came_ref, place_ref, inside_ref, emb_hbm, out_ref, emb_ref, sem):
    chips, cols = out_ref.shape[0], out_ref.shape[1] // CORES
    rows = chips * SLOTS
    summed = most_ref[...] + came_ref[...].astype(F32)
    unit = summed * lax.rsqrt(jnp.sum(summed * summed, axis=-1, keepdims=True) + 1e-06)
    emb_ref[...] = unit
    emb_out = pltpu.make_async_copy(emb_ref, emb_hbm, sem)
    emb_out.start()
    place = place_ref[...]
    moved = jnp.dot(place, unit.astype(BF), preferred_element_type=F32).astype(BF)
    for core in range(CORES):
        for col in range(cols):
            block = moved[core * rows : (core + 1) * rows, col * LANES : (col + 1) * LANES]
            out_ref[:, core * cols + col] = block.reshape(chips, SLOTS, LANES)
    inside = jnp.dot(place, inside_ref[...], preferred_element_type=F32)
    lane = lax.broadcasted_iota(jnp.int32, (rows, LANES), 1)
    beside = jnp.where(lane < LANES // CORES, inside[:rows], inside[rows:])
    out_ref[:, CORES * cols] = beside.astype(BF).reshape(chips, SLOTS, LANES)
    emb_out.wait()


def combine_kernel(got_ref, mine_ref, other_ref):
    chips, cols = got_ref.shape[0], got_ref.shape[1] // CORES
    rows = chips * SLOTS
    part = LANES // CORES
    inside = got_ref[:, CORES * cols].reshape(rows, LANES).astype(F32)
    lane = lax.rem(lax.broadcasted_iota(jnp.int32, (rows, LANES), 1), part).astype(F32)
    member = jnp.where(inside == lane, 1.0, 0.0).astype(BF)
    sums = []
    for core in range(CORES):
        data = [got_ref[:, core * cols + col].reshape(rows, LANES) for col in range(cols)]
        both = lax.dot_general(
            member, jnp.concatenate(data, axis=1), (((0,), (0,)), ((), ())), preferred_element_type=F32
        )
        sums.append(both[core * part : core * part + CL_OWN])
    first = lax.axis_index("c") == 0
    mine_ref[...] = jnp.where(first, sums[0], sums[1])
    other_ref[...] = jnp.where(first, sums[1], sums[0])


def finish_kernel(mine_ref, mate_ref, out_ref):
    sums = mine_ref[...] + mate_ref[...]
    out_ref[...] = sums * lax.rsqrt(jnp.sum(sums * sums, axis=-1, keepdims=True) + 1e-06)


def shards(features, tile_rows, tile_labels, tile_values, cluster_ids):
    tiles, tile = tile_values.shape[:2]
    insts, width = features.shape
    labs = cluster_ids.shape[0]
    chips = lax.axis_size("x")
    owners = lax.axis_size(INST + LAB)
    cols = width // LANES
    smem = pl.BlockSpec(memory_space=pltpu.MemorySpace.SMEM)
    hbm = pl.BlockSpec(memory_space=pltpu.MemorySpace.HBM)
    tile_scratch = [pltpu.SMEM((tiles,), jnp.int32)] * 2 + [pltpu.VMEM(tile_values.shape, BF)]
    far_steps, near_steps = (2,), (0, 1, -1)

    def product_cost(steps):
        return pl.CostEstimate(
            flops=len(steps) * tile * tile * width * 2,
            bytes_accessed=2 * (tiles * tile * tile + insts * width + len(steps) * tile * width),
            transcendentals=0,
        )

    far_away, normed = pl.pallas_call(
        functools.partial(first_kernel, far_steps),
        grid=(1,),
        out_shape=(jax.ShapeDtypeStruct((tile, width), BF), jax.ShapeDtypeStruct((insts, width), BF)),
        in_specs=[hbm] * 4,
        out_specs=(full((tile, width)), full((insts, width))),
        scratch_shapes=tile_scratch
        + [pltpu.VMEM((insts, width), BF), pltpu.SemaphoreType.DMA((4,))],
        compiler_params=params(),
        cost_estimate=product_cost(far_steps),
        name="far_away",
    )(*(in_hbm(a) for a in (tile_rows, tile_labels, tile_values, features)))

    def later(name, x, *jobs):
        shapes = [(len(steps) * tile, width) for _, steps in jobs]
        return pl.pallas_call(
            functools.partial(later_kernel, jobs),
            grid=(1,),
            out_shape=[jax.ShapeDtypeStruct(shape, BF) for shape in shapes],
            in_specs=[smem] * 2 + [full(tile_values.shape), full((insts, width))],
            out_specs=[full(shape) for shape in shapes],
            compiler_params=params(),
            cost_estimate=product_cost(sum((steps for _, steps in jobs), ())),
            name=name,
        )(tile_rows, tile_labels, tile_values, x)

    def across(block):
        return lax.ppermute(block, "c", [(0, 1), (1, 0)])

    def along(block, step):
        pairs = [(i, i + step * (1 - 2 * c)) for i in range(chips) for c in range(CORES)]
        pairs = [(i * CORES + k % CORES, j % chips * CORES + k % CORES) for k, (i, j) in enumerate(pairs)]
        return lax.ppermute(block, INST, pairs)

    far_mate = across(far_away)
    far_own, near_away = later("far_own", normed, (False, far_steps), (True, near_steps))
    far = (far_own.astype(F32) + far_mate.astype(F32)).astype(BF)
    ids, normed, near_away, far = lax.optimization_barrier((cluster_ids, normed, near_away, far))
    far_came = along(far, 1)
    mate = across(near_away)
    (own,) = later("near_own", normed, (False, near_steps))

    def pair(k):
        return own[k * tile : (k + 1) * tile].astype(F32) + mate[k * tile : (k + 1) * tile].astype(F32)

    free_came = along(pair(2).astype(BF), -1)
    block = full((tile, width))
    loaded = pl.pallas_call(
        load_kernel,
        grid=(1,),
        out_shape=jax.ShapeDtypeStruct((tile, width), BF),
        in_specs=[pl.BlockSpec((tile, width), lambda *_: (1, 0))] * 2 + [block],
        out_specs=block,
        compiler_params=params(),
        name="load",
    )(own, mate, far_came)
    came = along(loaded, 1)
    most = pair(0) + free_came.astype(F32)
    place, inside = pl.pallas_call(
        functools.partial(route_kernel, lax.axis_size(LAB)),
        grid=(1,),
        out_shape=(jax.ShapeDtypeStruct((SLOTS * owners, labs), BF), jax.ShapeDtypeStruct((labs, LANES), BF)),
        in_specs=[full((1, labs))],
        out_specs=(full((SLOTS * owners, labs)), full((labs, LANES))),
        compiler_params=params(),
        name="route",
    )(ids.reshape(1, labs))
    block = full((tile, width))
    message = (owners // CORES, CORES * cols + 1, SLOTS, LANES)
    label_embed, rows = pl.pallas_call(
        pack_kernel,
        grid=(1,),
        out_shape=(jax.ShapeDtypeStruct((labs, width), F32), jax.ShapeDtypeStruct(message, BF)),
        in_specs=[block] * 2 + [full((SLOTS * owners, labs)), full((labs, LANES))],
        out_specs=(hbm, full(message)),
        scratch_shapes=[pltpu.VMEM((labs, width), F32), pltpu.SemaphoreType.DMA],
        compiler_params=params(),
        name="pack",
    )(most, came, place, inside)
    got = lax.all_to_all(rows, ("x",) + LAB, 0, 0, tiled=True)
    sums = jax.ShapeDtypeStruct((CL_OWN, width), F32)
    mine, other = pl.pallas_call(
        combine_kernel,
        grid=(1,),
        out_shape=(sums, sums),
        in_specs=[full(message)],
        out_specs=(full(sums.shape), full(sums.shape)),
        compiler_params=params(),
        name="combine",
    )(got)
    centroids = pl.pallas_call(
        finish_kernel,
        grid=(1,),
        out_shape=sums,
        in_specs=[full(sums.shape)] * 2,
        out_specs=full(sums.shape),
        compiler_params=params(),
        name="finish",
    )(mine, across(other))
    return label_embed, centroids


def solution(mesh):
    insts, labs = mesh.devices.shape
    cut = (insts // CORES, CORES, labs // Y_CHIPS, Y_CHIPS)
    return jax.shard_map(
        shards,
        mesh=Mesh(mesh.devices.reshape(cut), INST + LAB),
        in_specs=(P(INST, None), P(INST + LAB), P(INST + LAB), P(INST + LAB, None, None), P(LAB + INST)),
        out_specs=(P(LAB + INST, None), P(INST + LAB, None)),
        check_vma=False,
    )
```

```python
import functools

import jax
import jax.numpy as jnp
from jax import lax
from jax.experimental import pallas as pl
from jax.experimental.pallas import tpu as pltpu
from jax.sharding import Mesh
from jax.sharding import PartitionSpec as P

CL_OWN = 32
RT = 2
SLOTS = 2
LANES = 128
CORES = 2
Y_CHIPS = 4
INST = ("x", "c")
LAB = ("z", "y")
BF = jnp.bfloat16
F32 = jnp.float32


def full(shape):
    return pl.BlockSpec(shape, lambda *_: (0,) * len(shape))


def params(**kwargs):
    return pltpu.CompilerParams(vmem_limit_bytes=24 << 20, **kwargs)


def in_hbm(array):
    return pltpu.with_memory_space_constraint(array, pltpu.MemorySpace.HBM)


def tiles_in(rows_hbm, labs_hbm, vals_hbm, rows_ref, labs_ref, vals_ref, sems):
    pairs = ((rows_hbm, rows_ref), (labs_hbm, labs_ref), (vals_hbm, vals_ref))
    return [pltpu.make_async_copy(src, dst, sems.at[k]) for k, (src, dst) in enumerate(pairs)]


def times(values, x):
    return lax.dot_general(values, x, (((0,), (0,)), ((), ())), preferred_element_type=F32)


def product(other, steps, rows_ref, labs_ref, vals_ref, x_ref, out_ref):
    tiles, tile = vals_ref.shape[0], vals_ref.shape[1]
    chips = lax.axis_size("x")
    core = lax.axis_index("c")
    if other:
        core = 1 - core
    for k, step in enumerate(steps):
        lab = lax.rem(lax.axis_index("x") + step * (1 - 2 * core) + chips, chips) * CORES + core
        held = []
        for r in range(RT):
            n = jnp.int32(-1)
            for t in range(tiles):
                n = jnp.where((rows_ref[t] == r) & (labs_ref[t] == lab), t, n)
            held.append(n)
        top, low = held
        count = (top >= 0).astype(jnp.int32) + (low >= 0).astype(jnp.int32)
        one = jnp.maximum(top, low)
        where = jnp.where(top >= 0, 0, tile)
        spot = pl.ds(k * tile, tile)

        @pl.when(count == 0)
        def _(spot=spot):
            out_ref[spot, :] = jnp.zeros((tile, out_ref.shape[1]), BF)

        @pl.when(count == 1)
        def _(spot=spot, one=one, where=where):
            out_ref[spot, :] = times(vals_ref[one], x_ref[pl.ds(pl.multiple_of(where, tile), tile), :]).astype(BF)

        @pl.when(count == 2)
        def _(spot=spot, top=top, low=low):
            both = times(vals_ref[top], x_ref[:tile, :]) + times(vals_ref[low], x_ref[tile:, :])
            out_ref[spot, :] = both.astype(BF)


def first_kernel(
    steps, rows_hbm, labs_hbm, vals_hbm, feat_hbm, out_ref, x_ref, rows_ref, labs_ref, vals_ref, feat_ref, sems
):
    feat_in = pltpu.make_async_copy(feat_hbm, feat_ref, sems.at[3])
    copies = tiles_in(rows_hbm, labs_hbm, vals_hbm, rows_ref, labs_ref, vals_ref, sems)
    feat_in.start()
    for copy in copies:
        copy.start()
    feat_in.wait()
    f = feat_ref[...].astype(F32)
    x_ref[...] = (f * lax.rsqrt(jnp.sum(f * f, axis=-1, keepdims=True) + 1e-06)).astype(BF)
    for copy in copies:
        copy.wait()
    product(True, steps, rows_ref, labs_ref, vals_ref, x_ref, out_ref)


def later_kernel(jobs, rows_ref, labs_ref, vals_ref, x_ref, *out_refs):
    for (other, steps), out_ref in zip(jobs, out_refs):
        product(other, steps, rows_ref, labs_ref, vals_ref, x_ref, out_ref)


def route_kernel(n_lab, ids_ref, place_ref, inside_ref):
    rows, labs = place_ref.shape
    chips = lax.axis_size("x")
    ids = ids_ref[...]
    down = lax.broadcasted_iota(jnp.int32, (labs, labs), 0)
    across = lax.broadcasted_iota(jnp.int32, (labs, labs), 1)
    ids_down = jnp.sum(jnp.where(down == across, ids, 0), axis=1, keepdims=True)
    owner = ids // CL_OWN
    earlier = (ids_down // CL_OWN == owner) & (down < across)
    rank = jnp.sum(earlier.astype(jnp.int32), axis=0, keepdims=True)
    inst = owner // n_lab
    core = (inst + lax.axis_index("c")) % CORES
    chip = (inst // CORES + chips - lax.axis_index("x")) % chips
    row = ((core * chips + chip) * n_lab + owner % n_lab) * SLOTS + rank
    place_ref[...] = jnp.where(lax.broadcasted_iota(jnp.int32, (rows, labs), 0) == row, 1.0, 0.0).astype(BF)
    inside_ref[...] = jnp.broadcast_to((ids_down % CL_OWN).astype(F32), inside_ref.shape).astype(BF)


def load_kernel(own_ref, mate_ref, far_ref, out_ref):
    out_ref[...] = (own_ref[...].astype(F32) + mate_ref[...].astype(F32) + far_ref[...].astype(F32)).astype(BF)


def pack_kernel(most_ref, came_ref, place_ref, inside_ref, emb_hbm, out_ref, emb_ref, sem):
    dests, width = out_ref.shape[0], emb_ref.shape[1]
    cols = width // LANES
    owners = out_ref.shape[1] // cols
    rows = dests * SLOTS
    summed = most_ref[...] + came_ref[...].astype(F32)
    unit = summed * lax.rsqrt(jnp.sum(summed * summed, axis=-1, keepdims=True) + 1e-06)
    emb_ref[...] = unit
    emb_out = pltpu.make_async_copy(emb_ref, emb_hbm, sem)
    emb_out.start()
    place = place_ref[...]
    moved = jnp.dot(place, unit.astype(BF), preferred_element_type=F32).astype(BF)
    inside = jnp.dot(place, inside_ref[...], preferred_element_type=F32)
    spot = lax.broadcasted_iota(jnp.int32, (rows, LANES), 1) // (LANES // owners)
    beside = jnp.zeros((rows, LANES), F32)
    for q in range(owners):
        mine = slice(q * rows, (q + 1) * rows)
        for col in range(cols):
            block = moved[mine, col * LANES : (col + 1) * LANES]
            out_ref[:, q * cols + col] = block.reshape(dests, SLOTS, LANES)
        beside = jnp.where(spot == q, inside[mine], beside)
    out_ref[:, owners * cols] = beside.astype(BF).reshape(dests, SLOTS, LANES)
    emb_out.wait()


def combine_kernel(got_ref, keep_ref, away_ref):
    sources, width = got_ref.shape[0], keep_ref.shape[1]
    cols = width // LANES
    owners = got_ref.shape[1] // cols
    rows = sources * SLOTS
    inside = got_ref[:, owners * cols].reshape(rows, LANES).astype(F32)
    lane = lax.broadcasted_iota(jnp.int32, (rows, LANES), 1).astype(F32)
    for q in range(owners):
        at = q * (LANES // owners)
        member = jnp.where(inside[:, at : at + 1] == lane, 1.0, 0.0).astype(BF)
        data = jnp.concatenate([got_ref[:, q * cols + col].reshape(rows, LANES) for col in range(cols)], axis=1)
        sums = lax.dot_general(member, data, (((0,), (0,)), ((), ())), preferred_element_type=F32)[:CL_OWN]
        core, k = divmod(q, owners // CORES)
        if core == 0:
            keep_ref[k * CL_OWN : (k + 1) * CL_OWN, :] = sums
        else:
            away_ref[k * CL_OWN : (k + 1) * CL_OWN, :] = sums.astype(BF)


def finish_kernel(own_ref, a_ref, b_ref, c_ref, out_ref):
    sums = own_ref[...] + a_ref[...].astype(F32) + b_ref[...].astype(F32) + c_ref[...].astype(F32)
    out_ref[...] = sums * lax.rsqrt(jnp.sum(sums * sums, axis=-1, keepdims=True) + 1e-06)


def shards(features, tile_rows, tile_labels, tile_values, cluster_ids):
    tiles, tile = tile_values.shape[:2]
    insts, width = features.shape
    labs = cluster_ids.shape[0]
    chips = lax.axis_size("x")
    owners = lax.axis_size(INST + LAB)
    cols = width // LANES
    smem = pl.BlockSpec(memory_space=pltpu.MemorySpace.SMEM)
    hbm = pl.BlockSpec(memory_space=pltpu.MemorySpace.HBM)
    tile_scratch = [pltpu.SMEM((tiles,), jnp.int32)] * 2 + [pltpu.VMEM(tile_values.shape, BF)]
    far_steps, near_steps = (2,), (0, 1, -1)

    def product_cost(steps):
        return pl.CostEstimate(
            flops=len(steps) * tile * tile * width * 2,
            bytes_accessed=2 * (tiles * tile * tile + insts * width + len(steps) * tile * width),
            transcendentals=0,
        )

    far_away, normed = pl.pallas_call(
        functools.partial(first_kernel, far_steps),
        grid=(1,),
        out_shape=(jax.ShapeDtypeStruct((tile, width), BF), jax.ShapeDtypeStruct((insts, width), BF)),
        in_specs=[hbm] * 4,
        out_specs=(full((tile, width)), full((insts, width))),
        scratch_shapes=tile_scratch
        + [pltpu.VMEM((insts, width), BF), pltpu.SemaphoreType.DMA((4,))],
        compiler_params=params(),
        cost_estimate=product_cost(far_steps),
        name="far_away",
    )(*(in_hbm(a) for a in (tile_rows, tile_labels, tile_values, features)))

    def later(name, x, *jobs):
        shapes = [(len(steps) * tile, width) for _, steps in jobs]
        return pl.pallas_call(
            functools.partial(later_kernel, jobs),
            grid=(1,),
            out_shape=[jax.ShapeDtypeStruct(shape, BF) for shape in shapes],
            in_specs=[smem] * 2 + [full(tile_values.shape), full((insts, width))],
            out_specs=[full(shape) for shape in shapes],
            compiler_params=params(),
            cost_estimate=product_cost(sum((steps for _, steps in jobs), ())),
            name=name,
        )(tile_rows, tile_labels, tile_values, x)

    def across(block):
        return lax.ppermute(block, "c", [(0, 1), (1, 0)])

    def along(block, step):
        pairs = [(i, i + step * (1 - 2 * c)) for i in range(chips) for c in range(CORES)]
        pairs = [(i * CORES + k % CORES, j % chips * CORES + k % CORES) for k, (i, j) in enumerate(pairs)]
        return lax.ppermute(block, INST, pairs)

    far_mate = across(far_away)
    far_own, near_away = later("far_own", normed, (False, far_steps), (True, near_steps))
    far = (far_own.astype(F32) + far_mate.astype(F32)).astype(BF)
    ids, normed, near_away, far = lax.optimization_barrier((cluster_ids, normed, near_away, far))
    far_came = along(far, 1)
    mate = across(near_away)
    (own,) = later("near_own", normed, (False, near_steps))

    def pair(k):
        return own[k * tile : (k + 1) * tile].astype(F32) + mate[k * tile : (k + 1) * tile].astype(F32)

    free_came = along(pair(2).astype(BF), -1)
    block = full((tile, width))
    loaded = pl.pallas_call(
        load_kernel,
        grid=(1,),
        out_shape=jax.ShapeDtypeStruct((tile, width), BF),
        in_specs=[pl.BlockSpec((tile, width), lambda *_: (1, 0))] * 2 + [block],
        out_specs=block,
        compiler_params=params(),
        name="load",
    )(own, mate, far_came)
    came = along(loaded, 1)
    most = pair(0) + free_came.astype(F32)
    place, inside = pl.pallas_call(
        functools.partial(route_kernel, lax.axis_size(LAB)),
        grid=(1,),
        out_shape=(jax.ShapeDtypeStruct((SLOTS * owners, labs), BF), jax.ShapeDtypeStruct((labs, LANES), BF)),
        in_specs=[full((1, labs))],
        out_specs=(full((SLOTS * owners, labs)), full((labs, LANES))),
        compiler_params=params(),
        name="route",
    )(ids.reshape(1, labs))
    block = full((tile, width))
    message = (lax.axis_size(LAB), lax.axis_size(INST) * cols + 1, SLOTS, LANES)
    label_embed, rows = pl.pallas_call(
        pack_kernel,
        grid=(1,),
        out_shape=(jax.ShapeDtypeStruct((labs, width), F32), jax.ShapeDtypeStruct(message, BF)),
        in_specs=[block] * 2 + [full((SLOTS * owners, labs)), full((labs, LANES))],
        out_specs=(hbm, full(message)),
        scratch_shapes=[pltpu.VMEM((labs, width), F32), pltpu.SemaphoreType.DMA],
        compiler_params=params(),
        name="pack",
    )(most, came, place, inside)
    got = lax.all_to_all(rows, LAB, 0, 0, tiled=True)
    held = (chips * CL_OWN, width)
    keep, away = pl.pallas_call(
        combine_kernel,
        grid=(1,),
        out_shape=(jax.ShapeDtypeStruct(held, F32), jax.ShapeDtypeStruct(held, BF)),
        in_specs=[full(message)],
        out_specs=(full(held), full(held)),
        compiler_params=params(),
        name="combine",
    )(got)
    mate_sums = across(away)

    def cluster_sums(step):
        part = slice(step * CL_OWN, (step + 1) * CL_OWN)
        return keep[part] + mate_sums[part].astype(F32)

    sums_came = [
        lax.ppermute(cluster_sums(step).astype(BF), "x", [(i, (i + step) % chips) for i in range(chips)])
        for step in (2, 1, 3)
    ]
    block = full((CL_OWN, width))
    centroids = pl.pallas_call(
        finish_kernel,
        grid=(1,),
        out_shape=jax.ShapeDtypeStruct((CL_OWN, width), F32),
        in_specs=[block] * 4,
        out_specs=block,
        compiler_params=params(),
        name="finish",
    )(cluster_sums(0), *sums_came)
    return label_embed, centroids


def solution(mesh):
    insts, labs = mesh.devices.shape
    cut = (insts // CORES, CORES, labs // Y_CHIPS, Y_CHIPS)
    return jax.shard_map(
        shards,
        mesh=Mesh(mesh.devices.reshape(cut), INST + LAB),
        in_specs=(P(INST, None), P(INST + LAB), P(INST + LAB), P(INST + LAB, None, None), P(LAB + INST)),
        out_specs=(P(LAB + INST, None), P(INST + LAB, None)),
        check_vma=False,
    )
```

```python
import functools

import jax
import jax.numpy as jnp
from jax import lax
from jax.experimental import pallas as pl
from jax.experimental.pallas import tpu as pltpu
from jax.sharding import Mesh
from jax.sharding import PartitionSpec as P

CL_OWN = 32
RT = 2
SLOTS = 2
LANES = 128
CORES = 2
Y_CHIPS = 4
INST = ("x", "c")
LAB = ("z", "y")
BF = jnp.bfloat16
F32 = jnp.float32


def full(shape):
    return pl.BlockSpec(shape, lambda *_: (0,) * len(shape))


def params(**kwargs):
    return pltpu.CompilerParams(vmem_limit_bytes=24 << 20, **kwargs)


def in_hbm(array):
    return pltpu.with_memory_space_constraint(array, pltpu.MemorySpace.HBM)


def tiles_in(rows_hbm, labs_hbm, vals_hbm, rows_ref, labs_ref, vals_ref, sems):
    pairs = ((rows_hbm, rows_ref), (labs_hbm, labs_ref), (vals_hbm, vals_ref))
    return [pltpu.make_async_copy(src, dst, sems.at[k]) for k, (src, dst) in enumerate(pairs)]


def times(values, x):
    return lax.dot_general(values, x, (((0,), (0,)), ((), ())), preferred_element_type=F32)


def product(other, steps, rows_ref, labs_ref, vals_ref, x_ref, out_ref):
    tiles, tile = vals_ref.shape[0], vals_ref.shape[1]
    chips = lax.axis_size("x")
    core = lax.axis_index("c")
    if other:
        core = 1 - core
    for k, step in enumerate(steps):
        lab = lax.rem(lax.axis_index("x") + step * (1 - 2 * core) + chips, chips) * CORES + core
        held = []
        for r in range(RT):
            n = jnp.int32(-1)
            for t in range(tiles):
                n = jnp.where((rows_ref[t] == r) & (labs_ref[t] == lab), t, n)
            held.append(n)
        top, low = held
        count = (top >= 0).astype(jnp.int32) + (low >= 0).astype(jnp.int32)
        one = jnp.maximum(top, low)
        where = jnp.where(top >= 0, 0, tile)
        spot = pl.ds(k * tile, tile)

        @pl.when(count == 0)
        def _(spot=spot):
            out_ref[spot, :] = jnp.zeros((tile, out_ref.shape[1]), BF)

        @pl.when(count == 1)
        def _(spot=spot, one=one, where=where):
            out_ref[spot, :] = times(vals_ref[one], x_ref[pl.ds(pl.multiple_of(where, tile), tile), :]).astype(BF)

        @pl.when(count == 2)
        def _(spot=spot, top=top, low=low):
            both = times(vals_ref[top], x_ref[:tile, :]) + times(vals_ref[low], x_ref[tile:, :])
            out_ref[spot, :] = both.astype(BF)


def first_kernel(
    steps, rows_hbm, labs_hbm, vals_hbm, feat_hbm, out_ref, x_ref, rows_ref, labs_ref, vals_ref, feat_ref, sems
):
    feat_in = pltpu.make_async_copy(feat_hbm, feat_ref, sems.at[3])
    copies = tiles_in(rows_hbm, labs_hbm, vals_hbm, rows_ref, labs_ref, vals_ref, sems)
    feat_in.start()
    for copy in copies:
        copy.start()
    feat_in.wait()
    f = feat_ref[...].astype(F32)
    x_ref[...] = (f * lax.rsqrt(jnp.sum(f * f, axis=-1, keepdims=True) + 1e-06)).astype(BF)
    for copy in copies:
        copy.wait()
    product(True, steps, rows_ref, labs_ref, vals_ref, x_ref, out_ref)


def later_kernel(jobs, rows_ref, labs_ref, vals_ref, x_ref, *out_refs):
    for (other, steps), out_ref in zip(jobs, out_refs):
        product(other, steps, rows_ref, labs_ref, vals_ref, x_ref, out_ref)


def route_kernel(n_lab, ids_ref, place_ref, inside_ref):
    rows, labs = place_ref.shape
    chips = lax.axis_size("x")
    ids = ids_ref[...]
    down = lax.broadcasted_iota(jnp.int32, (labs, labs), 0)
    across = lax.broadcasted_iota(jnp.int32, (labs, labs), 1)
    ids_down = jnp.sum(jnp.where(down == across, ids, 0), axis=1, keepdims=True)
    owner = ids // CL_OWN
    earlier = (ids_down // CL_OWN == owner) & (down < across)
    rank = jnp.sum(earlier.astype(jnp.int32), axis=0, keepdims=True)
    inst = owner // n_lab
    core = (inst + lax.axis_index("c")) % CORES
    chip = inst // CORES ^ lax.axis_index("x")
    row = ((core * chips + chip) * n_lab + owner % n_lab) * SLOTS + rank
    place_ref[...] = jnp.where(lax.broadcasted_iota(jnp.int32, (rows, labs), 0) == row, 1.0, 0.0).astype(BF)
    inside_ref[...] = jnp.broadcast_to((ids_down % CL_OWN).astype(F32), inside_ref.shape).astype(BF)


def load_kernel(own_ref, mate_ref, far_ref, out_ref):
    out_ref[...] = (own_ref[...].astype(F32) + mate_ref[...].astype(F32) + far_ref[...].astype(F32)).astype(BF)


def pack_kernel(most_ref, came_ref, place_ref, inside_ref, emb_hbm, out_ref, emb_ref, sem):
    dests, width = out_ref.shape[0], emb_ref.shape[1]
    cols = width // LANES
    owners = out_ref.shape[1] // cols
    rows = dests * SLOTS
    summed = most_ref[...] + came_ref[...].astype(F32)
    unit = summed * lax.rsqrt(jnp.sum(summed * summed, axis=-1, keepdims=True) + 1e-06)
    emb_ref[...] = unit
    emb_out = pltpu.make_async_copy(emb_ref, emb_hbm, sem)
    emb_out.start()
    place = place_ref[...]
    moved = jnp.dot(place, unit.astype(BF), preferred_element_type=F32).astype(BF)
    inside = jnp.dot(place, inside_ref[...], preferred_element_type=F32)
    spot = lax.broadcasted_iota(jnp.int32, (rows, LANES), 1) // (LANES // owners)
    beside = jnp.zeros((rows, LANES), F32)
    for q in range(owners):
        mine = slice(q * rows, (q + 1) * rows)
        for col in range(cols):
            block = moved[mine, col * LANES : (col + 1) * LANES]
            out_ref[:, q * cols + col] = block.reshape(dests, SLOTS, LANES)
        beside = jnp.where(spot == q, inside[mine], beside)
    out_ref[:, owners * cols] = beside.astype(BF).reshape(dests, SLOTS, LANES)
    emb_out.wait()


def combine_kernel(got_ref, keep_ref, away_ref):
    sources, width = got_ref.shape[0], keep_ref.shape[1]
    cols = width // LANES
    owners = got_ref.shape[1] // cols
    rows = sources * SLOTS
    inside = got_ref[:, owners * cols].reshape(rows, LANES).astype(F32)
    lane = lax.broadcasted_iota(jnp.int32, (rows, LANES), 1).astype(F32)
    for q in range(owners):
        at = q * (LANES // owners)
        member = jnp.where(inside[:, at : at + 1] == lane, 1.0, 0.0).astype(BF)
        data = jnp.concatenate([got_ref[:, q * cols + col].reshape(rows, LANES) for col in range(cols)], axis=1)
        sums = lax.dot_general(member, data, (((0,), (0,)), ((), ())), preferred_element_type=F32)[:CL_OWN]
        core, k = divmod(q, owners // CORES)
        if core == 0:
            keep_ref[k * CL_OWN : (k + 1) * CL_OWN, :] = sums
        else:
            away_ref[k * CL_OWN : (k + 1) * CL_OWN, :] = sums.astype(BF)


def finish_kernel(own_ref, came_ref, out_ref):
    sums = own_ref[...] + came_ref[...].astype(F32)
    out_ref[...] = sums * lax.rsqrt(jnp.sum(sums * sums, axis=-1, keepdims=True) + 1e-06)


def shards(features, tile_rows, tile_labels, tile_values, cluster_ids):
    tiles, tile = tile_values.shape[:2]
    insts, width = features.shape
    labs = cluster_ids.shape[0]
    chips = lax.axis_size("x")
    owners = lax.axis_size(INST + LAB)
    cols = width // LANES
    smem = pl.BlockSpec(memory_space=pltpu.MemorySpace.SMEM)
    hbm = pl.BlockSpec(memory_space=pltpu.MemorySpace.HBM)
    tile_scratch = [pltpu.SMEM((tiles,), jnp.int32)] * 2 + [pltpu.VMEM(tile_values.shape, BF)]
    far_steps, near_steps = (2,), (0, 1, -1)

    def product_cost(steps):
        return pl.CostEstimate(
            flops=len(steps) * tile * tile * width * 2,
            bytes_accessed=2 * (tiles * tile * tile + insts * width + len(steps) * tile * width),
            transcendentals=0,
        )

    far_away, normed = pl.pallas_call(
        functools.partial(first_kernel, far_steps),
        grid=(1,),
        out_shape=(jax.ShapeDtypeStruct((tile, width), BF), jax.ShapeDtypeStruct((insts, width), BF)),
        in_specs=[hbm] * 4,
        out_specs=(full((tile, width)), full((insts, width))),
        scratch_shapes=tile_scratch
        + [pltpu.VMEM((insts, width), BF), pltpu.SemaphoreType.DMA((4,))],
        compiler_params=params(),
        cost_estimate=product_cost(far_steps),
        name="far_away",
    )(*(in_hbm(a) for a in (tile_rows, tile_labels, tile_values, features)))

    def later(name, x, *jobs):
        shapes = [(len(steps) * tile, width) for _, steps in jobs]
        return pl.pallas_call(
            functools.partial(later_kernel, jobs),
            grid=(1,),
            out_shape=[jax.ShapeDtypeStruct(shape, BF) for shape in shapes],
            in_specs=[smem] * 2 + [full(tile_values.shape), full((insts, width))],
            out_specs=[full(shape) for shape in shapes],
            compiler_params=params(),
            cost_estimate=product_cost(sum((steps for _, steps in jobs), ())),
            name=name,
        )(tile_rows, tile_labels, tile_values, x)

    def across(block):
        return lax.ppermute(block, "c", [(0, 1), (1, 0)])

    def along(block, step):
        pairs = [(i, i + step * (1 - 2 * c)) for i in range(chips) for c in range(CORES)]
        pairs = [(i * CORES + k % CORES, j % chips * CORES + k % CORES) for k, (i, j) in enumerate(pairs)]
        return lax.ppermute(block, INST, pairs)

    far_mate = across(far_away)
    far_own, near_away = later("far_own", normed, (False, far_steps), (True, near_steps))
    far = (far_own.astype(F32) + far_mate.astype(F32)).astype(BF)
    ids, normed, near_away, far = lax.optimization_barrier((cluster_ids, normed, near_away, far))
    far_came = along(far, 1)
    mate = across(near_away)
    (own,) = later("near_own", normed, (False, near_steps))

    def pair(k):
        return own[k * tile : (k + 1) * tile].astype(F32) + mate[k * tile : (k + 1) * tile].astype(F32)

    free_came = along(pair(2).astype(BF), -1)
    block = full((tile, width))
    loaded = pl.pallas_call(
        load_kernel,
        grid=(1,),
        out_shape=jax.ShapeDtypeStruct((tile, width), BF),
        in_specs=[pl.BlockSpec((tile, width), lambda *_: (1, 0))] * 2 + [block],
        out_specs=block,
        compiler_params=params(),
        name="load",
    )(own, mate, far_came)
    came = along(loaded, 1)
    most = pair(0) + free_came.astype(F32)
    place, inside = pl.pallas_call(
        functools.partial(route_kernel, lax.axis_size(LAB)),
        grid=(1,),
        out_shape=(jax.ShapeDtypeStruct((SLOTS * owners, labs), BF), jax.ShapeDtypeStruct((labs, LANES), BF)),
        in_specs=[full((1, labs))],
        out_specs=(full((SLOTS * owners, labs)), full((labs, LANES))),
        compiler_params=params(),
        name="route",
    )(ids.reshape(1, labs))
    block = full((tile, width))
    message = (lax.axis_size(LAB), lax.axis_size(INST) * cols + 1, SLOTS, LANES)
    label_embed, rows = pl.pallas_call(
        pack_kernel,
        grid=(1,),
        out_shape=(jax.ShapeDtypeStruct((labs, width), F32), jax.ShapeDtypeStruct(message, BF)),
        in_specs=[block] * 2 + [full((SLOTS * owners, labs)), full((labs, LANES))],
        out_specs=(hbm, full(message)),
        scratch_shapes=[pltpu.VMEM((labs, width), F32), pltpu.SemaphoreType.DMA],
        compiler_params=params(),
        name="pack",
    )(most, came, place, inside)
    got = lax.all_to_all(rows, LAB, 0, 0, tiled=True)
    held = (chips * CL_OWN, width)
    keep, away = pl.pallas_call(
        combine_kernel,
        grid=(1,),
        out_shape=(jax.ShapeDtypeStruct(held, F32), jax.ShapeDtypeStruct(held, BF)),
        in_specs=[full(message)],
        out_specs=(full(held), full(held)),
        compiler_params=params(),
        name="combine",
    )(got)
    mate_sums = across(away)

    sums = keep + mate_sums.astype(F32)
    left = chips
    while left > 1:
        left //= 2
        cut = left * CL_OWN
        came = lax.ppermute(sums[cut:].astype(BF), "x", [(i, i ^ left) for i in range(chips)])
        sums = sums[:cut]
        if left > 1:
            sums = sums + came.astype(F32)
    block = full((CL_OWN, width))
    centroids = pl.pallas_call(
        finish_kernel,
        grid=(1,),
        out_shape=jax.ShapeDtypeStruct((CL_OWN, width), F32),
        in_specs=[block] * 2,
        out_specs=block,
        compiler_params=params(),
        name="finish",
    )(sums, came)
    return label_embed, centroids


def solution(mesh):
    insts, labs = mesh.devices.shape
    cut = (insts // CORES, CORES, labs // Y_CHIPS, Y_CHIPS)
    return jax.shard_map(
        shards,
        mesh=Mesh(mesh.devices.reshape(cut), INST + LAB),
        in_specs=(P(INST, None), P(INST + LAB), P(INST + LAB), P(INST + LAB, None, None), P(LAB + INST)),
        out_specs=(P(LAB + INST, None), P(INST + LAB, None)),
        check_vma=False,
    )
```

```python
import functools

import jax
import jax.numpy as jnp
from jax import lax
from jax.experimental import pallas as pl
from jax.experimental.pallas import tpu as pltpu
from jax.sharding import Mesh
from jax.sharding import PartitionSpec as P

CL_OWN = 32
RT = 2
SLOTS = 2
LANES = 128
CORES = 2
Y_CHIPS = 4
INST = ("x", "c")
LAB = ("z", "y")
BF = jnp.bfloat16
F32 = jnp.float32


def full(shape):
    return pl.BlockSpec(shape, lambda *_: (0,) * len(shape))


def params(**kwargs):
    return pltpu.CompilerParams(vmem_limit_bytes=24 << 20, **kwargs)


def in_hbm(array):
    return pltpu.with_memory_space_constraint(array, pltpu.MemorySpace.HBM)


def tiles_in(rows_hbm, labs_hbm, vals_hbm, rows_ref, labs_ref, vals_ref, sems):
    pairs = ((rows_hbm, rows_ref), (labs_hbm, labs_ref), (vals_hbm, vals_ref))
    return [pltpu.make_async_copy(src, dst, sems.at[k]) for k, (src, dst) in enumerate(pairs)]


def times(values, x):
    return lax.dot_general(values, x, (((0,), (0,)), ((), ())), preferred_element_type=F32)


def product(other, steps, rows_ref, labs_ref, vals_ref, x_ref, out_ref):
    tiles, tile = vals_ref.shape[0], vals_ref.shape[1]
    chips = lax.axis_size("x")
    core = lax.axis_index("c")
    if other:
        core = 1 - core
    for k, step in enumerate(steps):
        lab = lax.rem(lax.axis_index("x") + step * (1 - 2 * core) + chips, chips) * CORES + core
        held = []
        for r in range(RT):
            n = jnp.int32(-1)
            for t in range(tiles):
                n = jnp.where((rows_ref[t] == r) & (labs_ref[t] == lab), t, n)
            held.append(n)
        top, low = held
        count = (top >= 0).astype(jnp.int32) + (low >= 0).astype(jnp.int32)
        one = jnp.maximum(top, low)
        where = jnp.where(top >= 0, 0, tile)
        spot = pl.ds(k * tile, tile)

        @pl.when(count == 0)
        def _(spot=spot):
            out_ref[spot, :] = jnp.zeros((tile, out_ref.shape[1]), BF)

        @pl.when(count == 1)
        def _(spot=spot, one=one, where=where):
            out_ref[spot, :] = times(vals_ref[one], x_ref[pl.ds(pl.multiple_of(where, tile), tile), :]).astype(BF)

        @pl.when(count == 2)
        def _(spot=spot, top=top, low=low):
            both = times(vals_ref[top], x_ref[:tile, :]) + times(vals_ref[low], x_ref[tile:, :])
            out_ref[spot, :] = both.astype(BF)


def first_kernel(
    steps, rows_hbm, labs_hbm, vals_hbm, feat_hbm, out_ref, x_ref, rows_ref, labs_ref, vals_ref, feat_ref, sems
):
    tile = vals_ref.shape[1]
    halves = [slice(r * tile, (r + 1) * tile) for r in range(RT)]
    feats = [pltpu.make_async_copy(feat_hbm.at[h], feat_ref.at[h], sems.at[3 + r]) for r, h in enumerate(halves)]
    copies = tiles_in(rows_hbm, labs_hbm, vals_hbm, rows_ref, labs_ref, vals_ref, sems)
    for copy in feats + copies:
        copy.start()
    for copy, h in zip(feats, halves):
        copy.wait()
        f = feat_ref[h, :].astype(F32)
        x_ref[h, :] = (f * lax.rsqrt(jnp.sum(f * f, axis=-1, keepdims=True) + 1e-06)).astype(BF)
    for copy in copies:
        copy.wait()
    product(True, steps, rows_ref, labs_ref, vals_ref, x_ref, out_ref)


def later_kernel(jobs, rows_ref, labs_ref, vals_ref, x_ref, *out_refs):
    for (other, steps), out_ref in zip(jobs, out_refs):
        product(other, steps, rows_ref, labs_ref, vals_ref, x_ref, out_ref)


def route_kernel(n_lab, ids_ref, place_ref, beside_ref):
    rows, labs = place_ref.shape
    ids = ids_ref[...]
    down = lax.broadcasted_iota(jnp.int32, (labs, labs), 0)
    across = lax.broadcasted_iota(jnp.int32, (labs, labs), 1)
    ids_down = jnp.sum(jnp.where(down == across, ids, 0), axis=1, keepdims=True)
    owner = ids // CL_OWN
    earlier = (ids_down // CL_OWN == owner) & (down < across)
    rank = jnp.sum(earlier.astype(jnp.int32), axis=0, keepdims=True)
    core = owner // n_lab % CORES
    chip = owner // (n_lab * CORES) * n_lab + owner % n_lab
    row = core * (rows // CORES) + chip * SLOTS + rank
    place = jnp.where(lax.broadcasted_iota(jnp.int32, (rows, labs), 0) == row, 1.0, 0.0).astype(BF)
    place_ref[...] = place
    inside = jnp.broadcast_to((ids_down % CL_OWN).astype(F32), (labs, LANES)).astype(BF)
    inside = jnp.dot(place, inside, preferred_element_type=F32)
    half = rows // CORES
    lane = lax.broadcasted_iota(jnp.int32, (half, LANES), 1)
    beside_ref[...] = jnp.where(lane < LANES // CORES, inside[:half], inside[half:]).astype(BF)


def load_kernel(own_ref, mate_ref, far_ref, out_ref):
    out_ref[...] = (own_ref[...].astype(F32) + mate_ref[...].astype(F32) + far_ref[...].astype(F32)).astype(BF)


def pack_kernel(most_ref, came_ref, place_ref, beside_ref, emb_hbm, out_ref, emb_ref, sems):
    chips, cols = out_ref.shape[0], out_ref.shape[1] // CORES
    rows = chips * SLOTS
    half = emb_ref.shape[0] // 2
    units, copies = [], []
    for k in range(2):
        part = slice(k * half, (k + 1) * half)
        summed = most_ref[part, :] + came_ref[part, :].astype(F32)
        unit = summed * lax.rsqrt(jnp.sum(summed * summed, axis=-1, keepdims=True) + 1e-06)
        emb_ref[part, :] = unit
        copies.append(pltpu.make_async_copy(emb_ref.at[part], emb_hbm.at[part], sems.at[k]))
        copies[k].start()
        units.append(unit.astype(BF))
    moved = jnp.dot(place_ref[...], jnp.concatenate(units, axis=0), preferred_element_type=F32).astype(BF)
    for core in range(CORES):
        for col in range(cols):
            block = moved[core * rows : (core + 1) * rows, col * LANES : (col + 1) * LANES]
            out_ref[:, core * cols + col] = block.reshape(chips, SLOTS, LANES)
    out_ref[:, CORES * cols] = beside_ref[...].reshape(chips, SLOTS, LANES)
    for copy in copies:
        copy.wait()


def combine_kernel(got_ref, mine_ref, other_ref):
    chips, cols = got_ref.shape[0], got_ref.shape[1] // CORES
    rows = chips * SLOTS
    part = LANES // CORES
    inside = got_ref[:, CORES * cols].reshape(rows, LANES).astype(F32)
    lane = lax.rem(lax.broadcasted_iota(jnp.int32, (rows, LANES), 1), part).astype(F32)
    member = jnp.where(inside == lane, 1.0, 0.0).astype(BF)
    sums = []
    for core in range(CORES):
        data = [got_ref[:, core * cols + col].reshape(rows, LANES) for col in range(cols)]
        both = lax.dot_general(
            member, jnp.concatenate(data, axis=1), (((0,), (0,)), ((), ())), preferred_element_type=F32
        )
        sums.append(both[core * part : core * part + CL_OWN])
    first = lax.axis_index("c") == 0
    mine_ref[...] = jnp.where(first, sums[0], sums[1])
    other_ref[...] = jnp.where(first, sums[1], sums[0])


def finish_kernel(mine_ref, mate_ref, out_ref):
    sums = mine_ref[...] + mate_ref[...]
    out_ref[...] = sums * lax.rsqrt(jnp.sum(sums * sums, axis=-1, keepdims=True) + 1e-06)


def shards(features, tile_rows, tile_labels, tile_values, cluster_ids):
    tiles, tile = tile_values.shape[:2]
    insts, width = features.shape
    labs = cluster_ids.shape[0]
    chips = lax.axis_size("x")
    owners = lax.axis_size(INST + LAB)
    cols = width // LANES
    smem = pl.BlockSpec(memory_space=pltpu.MemorySpace.SMEM)
    hbm = pl.BlockSpec(memory_space=pltpu.MemorySpace.HBM)
    tile_scratch = [pltpu.SMEM((tiles,), jnp.int32)] * 2 + [pltpu.VMEM(tile_values.shape, BF)]
    far_steps, near_steps = (2,), (0, 1, -1)

    def product_cost(steps):
        return pl.CostEstimate(
            flops=len(steps) * tile * tile * width * 2,
            bytes_accessed=2 * (tiles * tile * tile + insts * width + len(steps) * tile * width),
            transcendentals=0,
        )

    far_away, normed = pl.pallas_call(
        functools.partial(first_kernel, far_steps),
        grid=(1,),
        out_shape=(jax.ShapeDtypeStruct((tile, width), BF), jax.ShapeDtypeStruct((insts, width), BF)),
        in_specs=[hbm] * 4,
        out_specs=(full((tile, width)), full((insts, width))),
        scratch_shapes=tile_scratch
        + [pltpu.VMEM((insts, width), BF), pltpu.SemaphoreType.DMA((3 + RT,))],
        compiler_params=params(),
        cost_estimate=product_cost(far_steps),
        name="far_away",
    )(*(in_hbm(a) for a in (tile_rows, tile_labels, tile_values, features)))

    def later(name, x, *jobs):
        shapes = [(len(steps) * tile, width) for _, steps in jobs]
        return pl.pallas_call(
            functools.partial(later_kernel, jobs),
            grid=(1,),
            out_shape=[jax.ShapeDtypeStruct(shape, BF) for shape in shapes],
            in_specs=[smem] * 2 + [full(tile_values.shape), full((insts, width))],
            out_specs=[full(shape) for shape in shapes],
            compiler_params=params(),
            cost_estimate=product_cost(sum((steps for _, steps in jobs), ())),
            name=name,
        )(tile_rows, tile_labels, tile_values, x)

    def across(block):
        return lax.ppermute(block, "c", [(0, 1), (1, 0)])

    def along(block, step):
        pairs = [(i, i + step * (1 - 2 * c)) for i in range(chips) for c in range(CORES)]
        pairs = [(i * CORES + k % CORES, j % chips * CORES + k % CORES) for k, (i, j) in enumerate(pairs)]
        return lax.ppermute(block, INST, pairs)

    far_mate = across(far_away)
    far_own, near_away = later("far_own", normed, (False, far_steps), (True, near_steps))
    far = (far_own.astype(F32) + far_mate.astype(F32)).astype(BF)
    ids, normed, near_away, far = lax.optimization_barrier((cluster_ids, normed, near_away, far))
    far_came = along(far, 1)
    mate = across(near_away)
    (own,) = later("near_own", normed, (False, near_steps))

    def pair(k):
        return own[k * tile : (k + 1) * tile].astype(F32) + mate[k * tile : (k + 1) * tile].astype(F32)

    free_came = along(pair(2).astype(BF), -1)
    block = full((tile, width))
    loaded = pl.pallas_call(
        load_kernel,
        grid=(1,),
        out_shape=jax.ShapeDtypeStruct((tile, width), BF),
        in_specs=[pl.BlockSpec((tile, width), lambda *_: (1, 0))] * 2 + [block],
        out_specs=block,
        compiler_params=params(),
        name="load",
    )(own, mate, far_came)
    came = along(loaded, 1)
    most = pair(0) + free_came.astype(F32)
    place, beside = pl.pallas_call(
        functools.partial(route_kernel, lax.axis_size(LAB)),
        grid=(1,),
        out_shape=(jax.ShapeDtypeStruct((SLOTS * owners, labs), BF), jax.ShapeDtypeStruct((owners, LANES), BF)),
        in_specs=[full((1, labs))],
        out_specs=(full((SLOTS * owners, labs)), full((owners, LANES))),
        compiler_params=params(),
        name="route",
    )(ids.reshape(1, labs))
    block = full((tile, width))
    message = (owners // CORES, CORES * cols + 1, SLOTS, LANES)
    label_embed, rows = pl.pallas_call(
        pack_kernel,
        grid=(1,),
        out_shape=(jax.ShapeDtypeStruct((labs, width), F32), jax.ShapeDtypeStruct(message, BF)),
        in_specs=[block] * 2 + [full((SLOTS * owners, labs)), full((owners, LANES))],
        out_specs=(hbm, full(message)),
        scratch_shapes=[pltpu.VMEM((labs, width), F32), pltpu.SemaphoreType.DMA((2,))],
        compiler_params=params(),
        name="pack",
    )(most, came, place, beside)
    got = lax.all_to_all(rows, ("x",) + LAB, 0, 0, tiled=True)
    sums = jax.ShapeDtypeStruct((CL_OWN, width), F32)
    mine, other = pl.pallas_call(
        combine_kernel,
        grid=(1,),
        out_shape=(sums, sums),
        in_specs=[full(message)],
        out_specs=(full(sums.shape), full(sums.shape)),
        compiler_params=params(),
        name="combine",
    )(got)
    centroids = pl.pallas_call(
        finish_kernel,
        grid=(1,),
        out_shape=sums,
        in_specs=[full(sums.shape)] * 2,
        out_specs=full(sums.shape),
        compiler_params=params(),
        name="finish",
    )(mine, across(other))
    return label_embed, centroids


def solution(mesh):
    insts, labs = mesh.devices.shape
    cut = (insts // CORES, CORES, labs // Y_CHIPS, Y_CHIPS)
    return jax.shard_map(
        shards,
        mesh=Mesh(mesh.devices.reshape(cut), INST + LAB),
        in_specs=(P(INST, None), P(INST + LAB), P(INST + LAB), P(INST + LAB, None, None), P(LAB + INST)),
        out_specs=(P(LAB + INST, None), P(INST + LAB, None)),
        check_vma=False,
    )
```

```python
import functools

import jax
import jax.numpy as jnp
from jax import lax
from jax.experimental import pallas as pl
from jax.experimental.pallas import tpu as pltpu
from jax.sharding import Mesh
from jax.sharding import PartitionSpec as P

CL_OWN = 32
RT = 2
SLOTS = 2
LANES = 128
CORES = 2
Y_CHIPS = 4
INST = ("x", "c")
LAB = ("z", "y")
BF = jnp.bfloat16
F32 = jnp.float32


def full(shape):
    return pl.BlockSpec(shape, lambda *_: (0,) * len(shape))


def params(**kwargs):
    return pltpu.CompilerParams(vmem_limit_bytes=24 << 20, **kwargs)


def in_hbm(array):
    return pltpu.with_memory_space_constraint(array, pltpu.MemorySpace.HBM)


def tiles_in(rows_hbm, labs_hbm, vals_hbm, rows_ref, labs_ref, vals_ref, sems):
    pairs = ((rows_hbm, rows_ref), (labs_hbm, labs_ref), (vals_hbm, vals_ref))
    return [pltpu.make_async_copy(src, dst, sems.at[k]) for k, (src, dst) in enumerate(pairs)]


def times(values, x):
    return lax.dot_general(values, x, (((0,), (0,)), ((), ())), preferred_element_type=F32)


def product(other, steps, rows_ref, labs_ref, vals_ref, x_ref, out_ref):
    tiles, tile = vals_ref.shape[0], vals_ref.shape[1]
    chips = lax.axis_size("x")
    core = lax.axis_index("c")
    if other:
        core = 1 - core
    for k, step in enumerate(steps):
        lab = lax.rem(lax.axis_index("x") + step * (1 - 2 * core) + chips, chips) * CORES + core
        held = []
        for r in range(RT):
            n = jnp.int32(-1)
            for t in range(tiles):
                n = jnp.where((rows_ref[t] == r) & (labs_ref[t] == lab), t, n)
            held.append(n)
        top, low = held
        count = (top >= 0).astype(jnp.int32) + (low >= 0).astype(jnp.int32)
        one = jnp.maximum(top, low)
        where = jnp.where(top >= 0, 0, tile)
        spot = pl.ds(k * tile, tile)

        @pl.when(count == 0)
        def _(spot=spot):
            out_ref[spot, :] = jnp.zeros((tile, out_ref.shape[1]), BF)

        @pl.when(count == 1)
        def _(spot=spot, one=one, where=where):
            out_ref[spot, :] = times(vals_ref[one], x_ref[pl.ds(pl.multiple_of(where, tile), tile), :]).astype(BF)

        @pl.when(count == 2)
        def _(spot=spot, top=top, low=low):
            both = times(vals_ref[top], x_ref[:tile, :]) + times(vals_ref[low], x_ref[tile:, :])
            out_ref[spot, :] = both.astype(BF)


def first_kernel(
    steps, rows_hbm, labs_hbm, vals_hbm, feat_hbm, out_ref, x_ref, vals_ref, rows_ref, labs_ref, feat_ref, sems
):
    tile = vals_ref.shape[1]
    halves = [slice(r * tile, (r + 1) * tile) for r in range(RT)]
    feats = [pltpu.make_async_copy(feat_hbm.at[h], feat_ref.at[h], sems.at[3 + r]) for r, h in enumerate(halves)]
    copies = tiles_in(rows_hbm, labs_hbm, vals_hbm, rows_ref, labs_ref, vals_ref, sems)
    for copy in feats + copies:
        copy.start()
    for copy, h in zip(feats, halves):
        copy.wait()
        f = feat_ref[h, :].astype(F32)
        x_ref[h, :] = (f * lax.rsqrt(jnp.sum(f * f, axis=-1, keepdims=True) + 1e-06)).astype(BF)
    for copy in copies:
        copy.wait()
    product(True, steps, rows_ref, labs_ref, vals_ref, x_ref, out_ref)


def later_kernel(jobs, rows_ref, labs_ref, vals_ref, x_ref, *out_refs):
    for (other, steps), out_ref in zip(jobs, out_refs):
        product(other, steps, rows_ref, labs_ref, vals_ref, x_ref, out_ref)


def route_kernel(n_lab, ids_ref, place_ref, beside_ref):
    rows, labs = place_ref.shape
    ids = ids_ref[...]
    down = lax.broadcasted_iota(jnp.int32, (labs, labs), 0)
    across = lax.broadcasted_iota(jnp.int32, (labs, labs), 1)
    ids_down = jnp.sum(jnp.where(down == across, ids, 0), axis=1, keepdims=True)
    owner = ids // CL_OWN
    earlier = (ids_down // CL_OWN == owner) & (down < across)
    rank = jnp.sum(earlier.astype(jnp.int32), axis=0, keepdims=True)
    core = owner // n_lab % CORES
    chip = owner // (n_lab * CORES) * n_lab + owner % n_lab
    row = core * (rows // CORES) + chip * SLOTS + rank
    place = jnp.where(lax.broadcasted_iota(jnp.int32, (rows, labs), 0) == row, 1.0, 0.0).astype(BF)
    place_ref[...] = place
    inside = jnp.broadcast_to((ids_down % CL_OWN).astype(F32), (labs, LANES)).astype(BF)
    inside = jnp.dot(place, inside, preferred_element_type=F32)
    half = rows // CORES
    lane = lax.broadcasted_iota(jnp.int32, (half, LANES), 1)
    beside_ref[...] = jnp.where(lane < LANES // CORES, inside[:half], inside[half:]).astype(BF)


def load_kernel(own_ref, mate_ref, far_ref, out_ref):
    out_ref[...] = (own_ref[...].astype(F32) + mate_ref[...].astype(F32) + far_ref[...].astype(F32)).astype(BF)


def pack_kernel(most_ref, came_ref, place_ref, beside_ref, emb_hbm, out_ref, emb_ref, sems):
    chips, cols = out_ref.shape[0], out_ref.shape[1] // CORES
    rows = chips * SLOTS
    half = emb_ref.shape[0] // 2
    units, copies = [], []
    for k in range(2):
        part = slice(k * half, (k + 1) * half)
        summed = most_ref[part, :] + came_ref[part, :].astype(F32)
        unit = summed * lax.rsqrt(jnp.sum(summed * summed, axis=-1, keepdims=True) + 1e-06)
        emb_ref[part, :] = unit
        copies.append(pltpu.make_async_copy(emb_ref.at[part], emb_hbm.at[part], sems.at[k]))
        copies[k].start()
        units.append(unit.astype(BF))
    moved = jnp.dot(place_ref[...], jnp.concatenate(units, axis=0), preferred_element_type=F32).astype(BF)
    for core in range(CORES):
        for col in range(cols):
            block = moved[core * rows : (core + 1) * rows, col * LANES : (col + 1) * LANES]
            out_ref[:, core * cols + col] = block.reshape(chips, SLOTS, LANES)
    out_ref[:, CORES * cols] = beside_ref[...].reshape(chips, SLOTS, LANES)
    for copy in copies:
        copy.wait()


def combine_kernel(got_ref, mine_ref, other_ref):
    chips, cols = got_ref.shape[0], got_ref.shape[1] // CORES
    rows = chips * SLOTS
    part = LANES // CORES
    inside = got_ref[:, CORES * cols].reshape(rows, LANES).astype(F32)
    lane = lax.rem(lax.broadcasted_iota(jnp.int32, (rows, LANES), 1), part).astype(F32)
    member = jnp.where(inside == lane, 1.0, 0.0).astype(BF)
    sums = []
    for core in range(CORES):
        data = [got_ref[:, core * cols + col].reshape(rows, LANES) for col in range(cols)]
        both = lax.dot_general(
            member, jnp.concatenate(data, axis=1), (((0,), (0,)), ((), ())), preferred_element_type=F32
        )
        sums.append(both[core * part : core * part + CL_OWN])
    first = lax.axis_index("c") == 0
    mine_ref[...] = jnp.where(first, sums[0], sums[1])
    other_ref[...] = jnp.where(first, sums[1], sums[0])


def finish_kernel(mine_ref, mate_ref, out_ref):
    sums = mine_ref[...] + mate_ref[...]
    out_ref[...] = sums * lax.rsqrt(jnp.sum(sums * sums, axis=-1, keepdims=True) + 1e-06)


def shards(features, tile_rows, tile_labels, tile_values, cluster_ids):
    tiles, tile = tile_values.shape[:2]
    insts, width = features.shape
    labs = cluster_ids.shape[0]
    chips = lax.axis_size("x")
    owners = lax.axis_size(INST + LAB)
    cols = width // LANES
    smem = pl.BlockSpec(memory_space=pltpu.MemorySpace.SMEM)
    hbm = pl.BlockSpec(memory_space=pltpu.MemorySpace.HBM)
    tile_scratch = [pltpu.SMEM((tiles,), jnp.int32)] * 2
    far_steps, near_steps = (2,), (0, 1, -1)

    def product_cost(steps):
        return pl.CostEstimate(
            flops=len(steps) * tile * tile * width * 2,
            bytes_accessed=2 * (tiles * tile * tile + insts * width + len(steps) * tile * width),
            transcendentals=0,
        )

    far_away, normed, tiles_held = pl.pallas_call(
        functools.partial(first_kernel, far_steps),
        grid=(1,),
        out_shape=(
            jax.ShapeDtypeStruct((tile, width), BF),
            jax.ShapeDtypeStruct((insts, width), BF),
            jax.ShapeDtypeStruct(tile_values.shape, BF),
        ),
        in_specs=[hbm] * 4,
        out_specs=(full((tile, width)), full((insts, width)), full(tile_values.shape)),
        scratch_shapes=tile_scratch
        + [pltpu.VMEM((insts, width), BF), pltpu.SemaphoreType.DMA((3 + RT,))],
        compiler_params=params(),
        cost_estimate=product_cost(far_steps),
        name="far_away",
    )(*(in_hbm(a) for a in (tile_rows, tile_labels, tile_values, features)))

    def later(name, x, *jobs):
        shapes = [(len(steps) * tile, width) for _, steps in jobs]
        return pl.pallas_call(
            functools.partial(later_kernel, jobs),
            grid=(1,),
            out_shape=[jax.ShapeDtypeStruct(shape, BF) for shape in shapes],
            in_specs=[smem] * 2 + [full(tile_values.shape), full((insts, width))],
            out_specs=[full(shape) for shape in shapes],
            compiler_params=params(),
            cost_estimate=product_cost(sum((steps for _, steps in jobs), ())),
            name=name,
        )(tile_rows, tile_labels, tiles_held, x)

    def across(block):
        return lax.ppermute(block, "c", [(0, 1), (1, 0)])

    def along(block, step):
        pairs = [(i, i + step * (1 - 2 * c)) for i in range(chips) for c in range(CORES)]
        pairs = [(i * CORES + k % CORES, j % chips * CORES + k % CORES) for k, (i, j) in enumerate(pairs)]
        return lax.ppermute(block, INST, pairs)

    far_mate = across(far_away)
    far_own, near_away = later("far_own", normed, (False, far_steps), (True, near_steps))
    far = (far_own.astype(F32) + far_mate.astype(F32)).astype(BF)
    ids, normed, near_away, far = lax.optimization_barrier((cluster_ids, normed, near_away, far))
    far_came = along(far, 1)
    mate = across(near_away)
    (own,) = later("near_own", normed, (False, near_steps))

    def pair(k):
        return own[k * tile : (k + 1) * tile].astype(F32) + mate[k * tile : (k + 1) * tile].astype(F32)

    free_came = along(pair(2).astype(BF), -1)
    block = full((tile, width))
    loaded = pl.pallas_call(
        load_kernel,
        grid=(1,),
        out_shape=jax.ShapeDtypeStruct((tile, width), BF),
        in_specs=[pl.BlockSpec((tile, width), lambda *_: (1, 0))] * 2 + [block],
        out_specs=block,
        compiler_params=params(),
        name="load",
    )(own, mate, far_came)
    came = along(loaded, 1)
    most = pair(0) + free_came.astype(F32)
    place, beside = pl.pallas_call(
        functools.partial(route_kernel, lax.axis_size(LAB)),
        grid=(1,),
        out_shape=(jax.ShapeDtypeStruct((SLOTS * owners, labs), BF), jax.ShapeDtypeStruct((owners, LANES), BF)),
        in_specs=[full((1, labs))],
        out_specs=(full((SLOTS * owners, labs)), full((owners, LANES))),
        compiler_params=params(),
        name="route",
    )(ids.reshape(1, labs))
    block = full((tile, width))
    message = (owners // CORES, CORES * cols + 1, SLOTS, LANES)
    label_embed, rows = pl.pallas_call(
        pack_kernel,
        grid=(1,),
        out_shape=(jax.ShapeDtypeStruct((labs, width), F32), jax.ShapeDtypeStruct(message, BF)),
        in_specs=[block] * 2 + [full((SLOTS * owners, labs)), full((owners, LANES))],
        out_specs=(hbm, full(message)),
        scratch_shapes=[pltpu.VMEM((labs, width), F32), pltpu.SemaphoreType.DMA((2,))],
        compiler_params=params(),
        name="pack",
    )(most, came, place, beside)
    got = lax.all_to_all(rows, ("x",) + LAB, 0, 0, tiled=True)
    sums = jax.ShapeDtypeStruct((CL_OWN, width), F32)
    mine, other = pl.pallas_call(
        combine_kernel,
        grid=(1,),
        out_shape=(sums, sums),
        in_specs=[full(message)],
        out_specs=(full(sums.shape), full(sums.shape)),
        compiler_params=params(),
        name="combine",
    )(got)
    centroids = pl.pallas_call(
        finish_kernel,
        grid=(1,),
        out_shape=sums,
        in_specs=[full(sums.shape)] * 2,
        out_specs=full(sums.shape),
        compiler_params=params(),
        name="finish",
    )(mine, across(other))
    return label_embed, centroids


def solution(mesh):
    insts, labs = mesh.devices.shape
    cut = (insts // CORES, CORES, labs // Y_CHIPS, Y_CHIPS)
    return jax.shard_map(
        shards,
        mesh=Mesh(mesh.devices.reshape(cut), INST + LAB),
        in_specs=(P(INST, None), P(INST + LAB), P(INST + LAB), P(INST + LAB, None, None), P(LAB + INST)),
        out_specs=(P(LAB + INST, None), P(INST + LAB, None)),
        check_vma=False,
    )
```

```python
import functools

import jax
import jax.numpy as jnp
from jax import lax
from jax.experimental import pallas as pl
from jax.experimental.pallas import tpu as pltpu
from jax.sharding import Mesh
from jax.sharding import PartitionSpec as P

CL_OWN = 32
RT = 2
SLOTS = 2
LANES = 128
CORES = 2
Y_CHIPS = 4
INST = ("x", "c")
LAB = ("z", "y")
BF = jnp.bfloat16
F32 = jnp.float32


def full(shape):
    return pl.BlockSpec(shape, lambda *_: (0,) * len(shape))


def params(**kwargs):
    return pltpu.CompilerParams(vmem_limit_bytes=24 << 20, **kwargs)


def in_hbm(array):
    return pltpu.with_memory_space_constraint(array, pltpu.MemorySpace.HBM)


def tiles_in(rows_hbm, labs_hbm, vals_hbm, rows_ref, labs_ref, vals_ref, sems):
    pairs = ((rows_hbm, rows_ref), (labs_hbm, labs_ref), (vals_hbm, vals_ref))
    return [pltpu.make_async_copy(src, dst, sems.at[k]) for k, (src, dst) in enumerate(pairs)]


def times(values, x):
    return lax.dot_general(values, x, (((0,), (0,)), ((), ())), preferred_element_type=F32)


def product(other, steps, rows_ref, labs_ref, vals_ref, x_ref, out_ref):
    tiles, tile = vals_ref.shape[0], vals_ref.shape[1]
    chips = lax.axis_size("x")
    core = lax.axis_index("c")
    if other:
        core = 1 - core
    for k, step in enumerate(steps):
        lab = lax.rem(lax.axis_index("x") + step * (1 - 2 * core) + chips, chips) * CORES + core
        held = []
        for r in range(RT):
            n = jnp.int32(-1)
            for t in range(tiles):
                n = jnp.where((rows_ref[t] == r) & (labs_ref[t] == lab), t, n)
            held.append(n)
        top, low = held
        count = (top >= 0).astype(jnp.int32) + (low >= 0).astype(jnp.int32)
        one = jnp.maximum(top, low)
        where = jnp.where(top >= 0, 0, tile)
        spot = pl.ds(k * tile, tile)

        @pl.when(count == 0)
        def _(spot=spot):
            out_ref[spot, :] = jnp.zeros((tile, out_ref.shape[1]), BF)

        @pl.when(count == 1)
        def _(spot=spot, one=one, where=where):
            out_ref[spot, :] = times(vals_ref[one], x_ref[pl.ds(pl.multiple_of(where, tile), tile), :]).astype(BF)

        @pl.when(count == 2)
        def _(spot=spot, top=top, low=low):
            both = times(vals_ref[top], x_ref[:tile, :]) + times(vals_ref[low], x_ref[tile:, :])
            out_ref[spot, :] = both.astype(BF)


def first_kernel(
    steps, rows_hbm, labs_hbm, vals_hbm, feat_hbm, out_ref, x_ref, vals_ref, rows_ref, labs_ref, feat_ref, sems
):
    tile = vals_ref.shape[1]
    halves = [slice(r * tile, (r + 1) * tile) for r in range(RT)]
    feats = [pltpu.make_async_copy(feat_hbm.at[h], feat_ref.at[h], sems.at[3 + r]) for r, h in enumerate(halves)]
    copies = tiles_in(rows_hbm, labs_hbm, vals_hbm, rows_ref, labs_ref, vals_ref, sems)
    for copy in feats + copies:
        copy.start()
    for copy, h in zip(feats, halves):
        copy.wait()
        f = feat_ref[h, :].astype(F32)
        x_ref[h, :] = (f * lax.rsqrt(jnp.sum(f * f, axis=-1, keepdims=True) + 1e-06)).astype(BF)
    for copy in copies:
        copy.wait()
    product(True, steps, rows_ref, labs_ref, vals_ref, x_ref, out_ref)


def later_kernel(jobs, rows_ref, labs_ref, vals_ref, x_ref, *out_refs):
    for (other, steps), out_ref in zip(jobs, out_refs):
        product(other, steps, rows_ref, labs_ref, vals_ref, x_ref, out_ref)


def route_kernel(n_lab, ids_ref, place_ref, beside_ref):
    rows, labs = place_ref.shape
    ids = ids_ref[...]
    down = lax.broadcasted_iota(jnp.int32, (labs, labs), 0)
    across = lax.broadcasted_iota(jnp.int32, (labs, labs), 1)
    ids_down = jnp.sum(jnp.where(down == across, ids, 0), axis=1, keepdims=True)
    owner = ids // CL_OWN
    earlier = (ids_down // CL_OWN == owner) & (down < across)
    rank = jnp.sum(earlier.astype(jnp.int32), axis=0, keepdims=True)
    core = owner // n_lab % CORES
    chip = owner // (n_lab * CORES) * n_lab + owner % n_lab
    row = core * (rows // CORES) + chip * SLOTS + rank
    place = jnp.where(lax.broadcasted_iota(jnp.int32, (rows, labs), 0) == row, 1.0, 0.0).astype(BF)
    place_ref[...] = place
    inside = jnp.broadcast_to((ids_down % CL_OWN).astype(F32), (labs, LANES)).astype(BF)
    inside = jnp.dot(place, inside, preferred_element_type=F32)
    half = rows // CORES
    lane = lax.broadcasted_iota(jnp.int32, (half, LANES), 1)
    beside_ref[...] = jnp.where(lane < LANES // CORES, inside[:half], inside[half:]).astype(BF)


def load_kernel(own_ref, mate_ref, far_ref, out_ref):
    out_ref[...] = (own_ref[...].astype(F32) + mate_ref[...].astype(F32) + far_ref[...].astype(F32)).astype(BF)


def pack_kernel(most_ref, came_ref, place_ref, beside_ref, emb_ref, out_ref):
    chips, cols = out_ref.shape[0], out_ref.shape[1] // CORES
    rows = chips * SLOTS
    summed = most_ref[...] + came_ref[...].astype(F32)
    unit = summed * lax.rsqrt(jnp.sum(summed * summed, axis=-1, keepdims=True) + 1e-06)
    emb_ref[...] = unit
    moved = jnp.dot(place_ref[...], unit.astype(BF), preferred_element_type=F32).astype(BF)
    for core in range(CORES):
        for col in range(cols):
            block = moved[core * rows : (core + 1) * rows, col * LANES : (col + 1) * LANES]
            out_ref[:, core * cols + col] = block.reshape(chips, SLOTS, LANES)
    out_ref[:, CORES * cols] = beside_ref[...].reshape(chips, SLOTS, LANES)


def emit_kernel(unit_ref, out_hbm, sem):
    copy = pltpu.make_async_copy(unit_ref, out_hbm, sem)
    copy.start()
    copy.wait()


def combine_kernel(got_ref, mine_ref, other_ref):
    chips, cols = got_ref.shape[0], got_ref.shape[1] // CORES
    rows = chips * SLOTS
    part = LANES // CORES
    inside = got_ref[:, CORES * cols].reshape(rows, LANES).astype(F32)
    lane = lax.rem(lax.broadcasted_iota(jnp.int32, (rows, LANES), 1), part).astype(F32)
    member = jnp.where(inside == lane, 1.0, 0.0).astype(BF)
    sums = []
    for core in range(CORES):
        data = [got_ref[:, core * cols + col].reshape(rows, LANES) for col in range(cols)]
        both = lax.dot_general(
            member, jnp.concatenate(data, axis=1), (((0,), (0,)), ((), ())), preferred_element_type=F32
        )
        sums.append(both[core * part : core * part + CL_OWN])
    first = lax.axis_index("c") == 0
    mine_ref[...] = jnp.where(first, sums[0], sums[1])
    other_ref[...] = jnp.where(first, sums[1], sums[0])


def finish_kernel(mine_ref, mate_ref, out_ref):
    sums = mine_ref[...] + mate_ref[...]
    out_ref[...] = sums * lax.rsqrt(jnp.sum(sums * sums, axis=-1, keepdims=True) + 1e-06)


def shards(features, tile_rows, tile_labels, tile_values, cluster_ids):
    tiles, tile = tile_values.shape[:2]
    insts, width = features.shape
    labs = cluster_ids.shape[0]
    chips = lax.axis_size("x")
    owners = lax.axis_size(INST + LAB)
    cols = width // LANES
    smem = pl.BlockSpec(memory_space=pltpu.MemorySpace.SMEM)
    hbm = pl.BlockSpec(memory_space=pltpu.MemorySpace.HBM)
    tile_scratch = [pltpu.SMEM((tiles,), jnp.int32)] * 2
    far_steps, near_steps = (2,), (0, 1, -1)

    def product_cost(steps):
        return pl.CostEstimate(
            flops=len(steps) * tile * tile * width * 2,
            bytes_accessed=2 * (tiles * tile * tile + insts * width + len(steps) * tile * width),
            transcendentals=0,
        )

    far_away, normed, tiles_held = pl.pallas_call(
        functools.partial(first_kernel, far_steps),
        grid=(1,),
        out_shape=(
            jax.ShapeDtypeStruct((tile, width), BF),
            jax.ShapeDtypeStruct((insts, width), BF),
            jax.ShapeDtypeStruct(tile_values.shape, BF),
        ),
        in_specs=[hbm] * 4,
        out_specs=(full((tile, width)), full((insts, width)), full(tile_values.shape)),
        scratch_shapes=tile_scratch
        + [pltpu.VMEM((insts, width), BF), pltpu.SemaphoreType.DMA((3 + RT,))],
        compiler_params=params(),
        cost_estimate=product_cost(far_steps),
        name="far_away",
    )(*(in_hbm(a) for a in (tile_rows, tile_labels, tile_values, features)))

    def later(name, x, *jobs):
        shapes = [(len(steps) * tile, width) for _, steps in jobs]
        return pl.pallas_call(
            functools.partial(later_kernel, jobs),
            grid=(1,),
            out_shape=[jax.ShapeDtypeStruct(shape, BF) for shape in shapes],
            in_specs=[smem] * 2 + [full(tile_values.shape), full((insts, width))],
            out_specs=[full(shape) for shape in shapes],
            compiler_params=params(),
            cost_estimate=product_cost(sum((steps for _, steps in jobs), ())),
            name=name,
        )(tile_rows, tile_labels, tiles_held, x)

    def across(block):
        return lax.ppermute(block, "c", [(0, 1), (1, 0)])

    def along(block, step):
        pairs = [(i, i + step * (1 - 2 * c)) for i in range(chips) for c in range(CORES)]
        pairs = [(i * CORES + k % CORES, j % chips * CORES + k % CORES) for k, (i, j) in enumerate(pairs)]
        return lax.ppermute(block, INST, pairs)

    far_mate = across(far_away)
    far_own, near_away = later("far_own", normed, (False, far_steps), (True, near_steps))
    far = (far_own.astype(F32) + far_mate.astype(F32)).astype(BF)
    ids, normed, near_away, far = lax.optimization_barrier((cluster_ids, normed, near_away, far))
    far_came = along(far, 1)
    mate = across(near_away)
    (own,) = later("near_own", normed, (False, near_steps))

    def pair(k):
        return own[k * tile : (k + 1) * tile].astype(F32) + mate[k * tile : (k + 1) * tile].astype(F32)

    free_came = along(pair(2).astype(BF), -1)
    block = full((tile, width))
    loaded = pl.pallas_call(
        load_kernel,
        grid=(1,),
        out_shape=jax.ShapeDtypeStruct((tile, width), BF),
        in_specs=[pl.BlockSpec((tile, width), lambda *_: (1, 0))] * 2 + [block],
        out_specs=block,
        compiler_params=params(),
        name="load",
    )(own, mate, far_came)
    came = along(loaded, 1)
    most = pair(0) + free_came.astype(F32)
    place, beside = pl.pallas_call(
        functools.partial(route_kernel, lax.axis_size(LAB)),
        grid=(1,),
        out_shape=(jax.ShapeDtypeStruct((SLOTS * owners, labs), BF), jax.ShapeDtypeStruct((owners, LANES), BF)),
        in_specs=[full((1, labs))],
        out_specs=(full((SLOTS * owners, labs)), full((owners, LANES))),
        compiler_params=params(),
        name="route",
    )(ids.reshape(1, labs))
    block = full((tile, width))
    message = (owners // CORES, CORES * cols + 1, SLOTS, LANES)
    unit, rows = pl.pallas_call(
        pack_kernel,
        grid=(1,),
        out_shape=(jax.ShapeDtypeStruct((labs, width), F32), jax.ShapeDtypeStruct(message, BF)),
        in_specs=[block] * 2 + [full((SLOTS * owners, labs)), full((owners, LANES))],
        out_specs=(full((labs, width)), full(message)),
        compiler_params=params(),
        name="pack",
    )(most, came, place, beside)
    got = lax.all_to_all(rows, ("x",) + LAB, 0, 0, tiled=True)
    sums = jax.ShapeDtypeStruct((CL_OWN, width), F32)
    mine, other = pl.pallas_call(
        combine_kernel,
        grid=(1,),
        out_shape=(sums, sums),
        in_specs=[full(message)],
        out_specs=(full(sums.shape), full(sums.shape)),
        compiler_params=params(),
        name="combine",
    )(got)
    other, unit = lax.optimization_barrier((other, unit))
    label_embed = pl.pallas_call(
        emit_kernel,
        grid=(1,),
        out_shape=jax.ShapeDtypeStruct((labs, width), F32),
        in_specs=[full((labs, width))],
        out_specs=hbm,
        scratch_shapes=[pltpu.SemaphoreType.DMA],
        compiler_params=params(),
        name="emit",
    )(unit)
    centroids = pl.pallas_call(
        finish_kernel,
        grid=(1,),
        out_shape=sums,
        in_specs=[full(sums.shape)] * 2,
        out_specs=full(sums.shape),
        compiler_params=params(),
        name="finish",
    )(mine, across(other))
    return label_embed, centroids


def solution(mesh):
    insts, labs = mesh.devices.shape
    cut = (insts // CORES, CORES, labs // Y_CHIPS, Y_CHIPS)
    return jax.shard_map(
        shards,
        mesh=Mesh(mesh.devices.reshape(cut), INST + LAB),
        in_specs=(P(INST, None), P(INST + LAB), P(INST + LAB), P(INST + LAB, None, None), P(LAB + INST)),
        out_specs=(P(LAB + INST, None), P(INST + LAB, None)),
        check_vma=False,
    )
```

```python
import functools

import jax
import jax.numpy as jnp
from jax import lax
from jax.experimental import pallas as pl
from jax.experimental.pallas import tpu as pltpu
from jax.sharding import Mesh
from jax.sharding import PartitionSpec as P

CL_OWN = 32
RT = 2
SLOTS = 2
LANES = 128
CORES = 2
Y_CHIPS = 4
INST = ("x", "c")
LAB = ("z", "y")
BF = jnp.bfloat16
F32 = jnp.float32


def full(shape):
    return pl.BlockSpec(shape, lambda *_: (0,) * len(shape))


def params(**kwargs):
    return pltpu.CompilerParams(vmem_limit_bytes=24 << 20, **kwargs)


def in_hbm(array):
    return pltpu.with_memory_space_constraint(array, pltpu.MemorySpace.HBM)


def tiles_in(rows_hbm, labs_hbm, vals_hbm, rows_ref, labs_ref, vals_ref, sems):
    pairs = ((rows_hbm, rows_ref), (labs_hbm, labs_ref), (vals_hbm, vals_ref))
    return [pltpu.make_async_copy(src, dst, sems.at[k]) for k, (src, dst) in enumerate(pairs)]


def times(values, x):
    return lax.dot_general(values, x, (((0,), (0,)), ((), ())), preferred_element_type=F32)


def product(other, steps, rows_ref, labs_ref, vals_ref, x_ref, out_ref):
    tiles, tile = vals_ref.shape[0], vals_ref.shape[1]
    chips = lax.axis_size("x")
    core = lax.axis_index("c")
    if other:
        core = 1 - core
    for k, step in enumerate(steps):
        lab = lax.rem(lax.axis_index("x") + step * (1 - 2 * core) + chips, chips) * CORES + core
        held = []
        for r in range(RT):
            n = jnp.int32(-1)
            for t in range(tiles):
                n = jnp.where((rows_ref[t] == r) & (labs_ref[t] == lab), t, n)
            held.append(n)
        top, low = held
        count = (top >= 0).astype(jnp.int32) + (low >= 0).astype(jnp.int32)
        one = jnp.maximum(top, low)
        where = jnp.where(top >= 0, 0, tile)
        spot = pl.ds(k * tile, tile)

        @pl.when(count == 0)
        def _(spot=spot):
            out_ref[spot, :] = jnp.zeros((tile, out_ref.shape[1]), BF)

        @pl.when(count == 1)
        def _(spot=spot, one=one, where=where):
            out_ref[spot, :] = times(vals_ref[one], x_ref[pl.ds(pl.multiple_of(where, tile), tile), :]).astype(BF)

        @pl.when(count == 2)
        def _(spot=spot, top=top, low=low):
            both = times(vals_ref[top], x_ref[:tile, :]) + times(vals_ref[low], x_ref[tile:, :])
            out_ref[spot, :] = both.astype(BF)


def first_kernel(
    steps, rows_hbm, labs_hbm, vals_hbm, feat_hbm, out_ref, x_ref, vals_ref, rows_ref, labs_ref, feat_ref, sems
):
    tile = vals_ref.shape[1]
    halves = [slice(r * tile, (r + 1) * tile) for r in range(RT)]
    feats = [pltpu.make_async_copy(feat_hbm.at[h], feat_ref.at[h], sems.at[3 + r]) for r, h in enumerate(halves)]
    copies = tiles_in(rows_hbm, labs_hbm, vals_hbm, rows_ref, labs_ref, vals_ref, sems)
    for copy in feats + copies:
        copy.start()
    for copy, h in zip(feats, halves):
        copy.wait()
        f = feat_ref[h, :].astype(F32)
        x_ref[h, :] = (f * lax.rsqrt(jnp.sum(f * f, axis=-1, keepdims=True) + 1e-06)).astype(BF)
    for copy in copies:
        copy.wait()
    product(True, steps, rows_ref, labs_ref, vals_ref, x_ref, out_ref)


def later_kernel(jobs, rows_ref, labs_ref, vals_ref, x_ref, *out_refs):
    for (other, steps), out_ref in zip(jobs, out_refs):
        product(other, steps, rows_ref, labs_ref, vals_ref, x_ref, out_ref)


def route_kernel(n_lab, ids_ref, place_ref, beside_ref):
    rows, labs = place_ref.shape
    ids = ids_ref[...]
    down = lax.broadcasted_iota(jnp.int32, (labs, labs), 0)
    across = lax.broadcasted_iota(jnp.int32, (labs, labs), 1)
    ids_down = jnp.sum(jnp.where(down == across, ids, 0), axis=1, keepdims=True)
    owner = ids // CL_OWN
    earlier = (ids_down // CL_OWN == owner) & (down < across)
    rank = jnp.sum(earlier.astype(jnp.int32), axis=0, keepdims=True)
    core = owner // n_lab % CORES
    chip = owner // (n_lab * CORES) * n_lab + owner % n_lab
    row = core * (rows // CORES) + chip * SLOTS + rank
    place = jnp.where(lax.broadcasted_iota(jnp.int32, (rows, labs), 0) == row, 1.0, 0.0).astype(BF)
    place_ref[...] = place
    inside = jnp.broadcast_to((ids_down % CL_OWN).astype(F32), (labs, LANES)).astype(BF)
    inside = jnp.dot(place, inside, preferred_element_type=F32)
    half = rows // CORES
    lane = lax.broadcasted_iota(jnp.int32, (half, LANES), 1)
    beside_ref[...] = jnp.where(lane < LANES // CORES, inside[:half], inside[half:]).astype(BF)


def load_kernel(own_ref, mate_ref, far_ref, out_ref):
    out_ref[...] = (own_ref[...].astype(F32) + mate_ref[...].astype(F32) + far_ref[...].astype(F32)).astype(BF)


def pack_kernel(most_ref, came_ref, place_ref, beside_ref, emb_hbm, out_ref, emb_ref, sems):
    chips, cols = out_ref.shape[0], out_ref.shape[1] // CORES
    rows = chips * SLOTS
    half = emb_ref.shape[0] // 2
    units, copies = [], []
    for k in range(2):
        part = slice(k * half, (k + 1) * half)
        summed = most_ref[part, :] + came_ref[part, :].astype(F32)
        unit = summed * lax.rsqrt(jnp.sum(summed * summed, axis=-1, keepdims=True) + 1e-06)
        emb_ref[part, :] = unit
        copies.append(pltpu.make_async_copy(emb_ref.at[part], emb_hbm.at[part], sems.at[k]))
        copies[k].start()
        units.append(unit.astype(BF))
    moved = jnp.dot(place_ref[...], jnp.concatenate(units, axis=0), preferred_element_type=F32).astype(BF)
    for core in range(CORES):
        for col in range(cols):
            block = moved[core * rows : (core + 1) * rows, col * LANES : (col + 1) * LANES]
            out_ref[:, core * cols + col] = block.reshape(chips, SLOTS, LANES)
    out_ref[:, CORES * cols] = beside_ref[...].reshape(chips, SLOTS, LANES)
    for copy in copies:
        copy.wait()


def combine_kernel(got_ref, mine_ref, other_ref):
    chips, cols = got_ref.shape[0], got_ref.shape[1] // CORES
    rows = chips * SLOTS
    part = LANES // CORES
    inside = got_ref[:, CORES * cols].reshape(rows, LANES).astype(F32)
    lane = lax.rem(lax.broadcasted_iota(jnp.int32, (rows, LANES), 1), part).astype(F32)
    member = jnp.where(inside == lane, 1.0, 0.0).astype(BF)
    sums = []
    for core in range(CORES):
        data = [got_ref[:, core * cols + col].reshape(rows, LANES) for col in range(cols)]
        both = lax.dot_general(
            member, jnp.concatenate(data, axis=1), (((0,), (0,)), ((), ())), preferred_element_type=F32
        )
        sums.append(both[core * part : core * part + CL_OWN])
    first = lax.axis_index("c") == 0
    mine_ref[...] = jnp.where(first, sums[0], sums[1])
    other_ref[...] = jnp.where(first, sums[1], sums[0]).astype(BF)


def finish_kernel(mine_ref, mate_ref, out_ref):
    sums = mine_ref[...] + mate_ref[...].astype(F32)
    out_ref[...] = sums * lax.rsqrt(jnp.sum(sums * sums, axis=-1, keepdims=True) + 1e-06)


def shards(features, tile_rows, tile_labels, tile_values, cluster_ids):
    tiles, tile = tile_values.shape[:2]
    insts, width = features.shape
    labs = cluster_ids.shape[0]
    chips = lax.axis_size("x")
    owners = lax.axis_size(INST + LAB)
    cols = width // LANES
    smem = pl.BlockSpec(memory_space=pltpu.MemorySpace.SMEM)
    hbm = pl.BlockSpec(memory_space=pltpu.MemorySpace.HBM)
    tile_scratch = [pltpu.SMEM((tiles,), jnp.int32)] * 2
    far_steps, near_steps = (2,), (0, 1, -1)

    def product_cost(steps):
        return pl.CostEstimate(
            flops=len(steps) * tile * tile * width * 2,
            bytes_accessed=2 * (tiles * tile * tile + insts * width + len(steps) * tile * width),
            transcendentals=0,
        )

    far_away, normed, tiles_held = pl.pallas_call(
        functools.partial(first_kernel, far_steps),
        grid=(1,),
        out_shape=(
            jax.ShapeDtypeStruct((tile, width), BF),
            jax.ShapeDtypeStruct((insts, width), BF),
            jax.ShapeDtypeStruct(tile_values.shape, BF),
        ),
        in_specs=[hbm] * 4,
        out_specs=(full((tile, width)), full((insts, width)), full(tile_values.shape)),
        scratch_shapes=tile_scratch
        + [pltpu.VMEM((insts, width), BF), pltpu.SemaphoreType.DMA((3 + RT,))],
        compiler_params=params(),
        cost_estimate=product_cost(far_steps),
        name="far_away",
    )(*(in_hbm(a) for a in (tile_rows, tile_labels, tile_values, features)))

    def later(name, x, *jobs):
        shapes = [(len(steps) * tile, width) for _, steps in jobs]
        return pl.pallas_call(
            functools.partial(later_kernel, jobs),
            grid=(1,),
            out_shape=[jax.ShapeDtypeStruct(shape, BF) for shape in shapes],
            in_specs=[smem] * 2 + [full(tile_values.shape), full((insts, width))],
            out_specs=[full(shape) for shape in shapes],
            compiler_params=params(),
            cost_estimate=product_cost(sum((steps for _, steps in jobs), ())),
            name=name,
        )(tile_rows, tile_labels, tiles_held, x)

    def across(block):
        return lax.ppermute(block, "c", [(0, 1), (1, 0)])

    def along(block, step):
        pairs = [(i, i + step * (1 - 2 * c)) for i in range(chips) for c in range(CORES)]
        pairs = [(i * CORES + k % CORES, j % chips * CORES + k % CORES) for k, (i, j) in enumerate(pairs)]
        return lax.ppermute(block, INST, pairs)

    far_mate = across(far_away)
    far_own, near_away = later("far_own", normed, (False, far_steps), (True, near_steps))
    far = (far_own.astype(F32) + far_mate.astype(F32)).astype(BF)
    ids, normed, near_away, far = lax.optimization_barrier((cluster_ids, normed, near_away, far))
    far_came = along(far, 1)
    mate = across(near_away)
    (own,) = later("near_own", normed, (False, near_steps))

    def pair(k):
        return own[k * tile : (k + 1) * tile].astype(F32) + mate[k * tile : (k + 1) * tile].astype(F32)

    free_came = along(pair(2).astype(BF), -1)
    block = full((tile, width))
    loaded = pl.pallas_call(
        load_kernel,
        grid=(1,),
        out_shape=jax.ShapeDtypeStruct((tile, width), BF),
        in_specs=[pl.BlockSpec((tile, width), lambda *_: (1, 0))] * 2 + [block],
        out_specs=block,
        compiler_params=params(),
        name="load",
    )(own, mate, far_came)
    came = along(loaded, 1)
    most = pair(0) + free_came.astype(F32)
    place, beside = pl.pallas_call(
        functools.partial(route_kernel, lax.axis_size(LAB)),
        grid=(1,),
        out_shape=(jax.ShapeDtypeStruct((SLOTS * owners, labs), BF), jax.ShapeDtypeStruct((owners, LANES), BF)),
        in_specs=[full((1, labs))],
        out_specs=(full((SLOTS * owners, labs)), full((owners, LANES))),
        compiler_params=params(),
        name="route",
    )(ids.reshape(1, labs))
    block = full((tile, width))
    message = (owners // CORES, CORES * cols + 1, SLOTS, LANES)
    label_embed, rows = pl.pallas_call(
        pack_kernel,
        grid=(1,),
        out_shape=(jax.ShapeDtypeStruct((labs, width), F32), jax.ShapeDtypeStruct(message, BF)),
        in_specs=[block] * 2 + [full((SLOTS * owners, labs)), full((owners, LANES))],
        out_specs=(hbm, full(message)),
        scratch_shapes=[pltpu.VMEM((labs, width), F32), pltpu.SemaphoreType.DMA((2,))],
        compiler_params=params(),
        name="pack",
    )(most, came, place, beside)
    got = lax.all_to_all(rows, ("x",) + LAB, 0, 0, tiled=True)
    sums = jax.ShapeDtypeStruct((CL_OWN, width), F32)
    mine, other = pl.pallas_call(
        combine_kernel,
        grid=(1,),
        out_shape=(sums, jax.ShapeDtypeStruct(sums.shape, BF)),
        in_specs=[full(message)],
        out_specs=(full(sums.shape), full(sums.shape)),
        compiler_params=params(),
        name="combine",
    )(got)
    centroids = pl.pallas_call(
        finish_kernel,
        grid=(1,),
        out_shape=sums,
        in_specs=[full(sums.shape)] * 2,
        out_specs=full(sums.shape),
        compiler_params=params(),
        name="finish",
    )(mine, across(other))
    return label_embed, centroids


def solution(mesh):
    insts, labs = mesh.devices.shape
    cut = (insts // CORES, CORES, labs // Y_CHIPS, Y_CHIPS)
    return jax.shard_map(
        shards,
        mesh=Mesh(mesh.devices.reshape(cut), INST + LAB),
        in_specs=(P(INST, None), P(INST + LAB), P(INST + LAB), P(INST + LAB, None, None), P(LAB + INST)),
        out_specs=(P(LAB + INST, None), P(INST + LAB, None)),
        check_vma=False,
    )
```
